256 devices in a mesh: tm: 16 (over z, core), space: 16 (over y, x).
Axes of the slice: x: 4, y: 4, z: 8, core: 2. Of those that a mesh axis runs over, the one named last changes fastest.
Arguments:
- starts: float32 [16, 192, 64, 128], P('tm', 'space'), may hold values from -45 to 45
- vel_x: float32 [192, 64, 128], P('space'), may hold values from -0.15 to 0.15
- vel_y: float32 [192, 64, 128], P('space'), may hold values from -0.15 to 0.15
- vel_z: float32 [192, 64, 128], P('space'), may hold values from -0.5 to 0.5
- kappa: float32 [192, 64, 128], P('space'), may hold values from 0.01 to 0.03
Outputs:
- new_starts: float32 [16, 192, 64, 128], P('tm', 'space')
- change_norm: float32 [], replicated
The draws below stay inside these ranges and needn't reach their ends.
All inputs are finite; a program needn't handle non-finite values.
Results may differ from the reference program's by a relative error of at most 0.0003.
Values sent between devices are 32-bit elements; how exact they have to be, the bound alone decides.
No kernel may reach another device: no remote copies, remote signals or barrier semaphores. Data moves between devices by JAX's collectives and lax.ppermute only.
A program may use at most 128 MiB of HBM per device.

```python
import math
import jax
import jax.numpy as jnp
from jax import lax

NX = 128
NY = 64
FSTEPS = 6
GC = 2
NZ = 192
SLICES = 16


def draw_starts(key, part):
    key_base = jax.random.fold_in(key, 11)
    key_rows = jax.random.fold_in(key, 12)
    key_cols = jax.random.fold_in(key, 13)
    shape = (SLICES, NZ, NY, NX)
    slice_pos = jnp.arange(SLICES, dtype=jnp.float32) / max(SLICES - 1, 1)
    depth_pos = jnp.arange(NZ, dtype=jnp.float32) / max(NZ - 1, 1)
    amplitude = jnp.sqrt((1.0 + 3.0 * slice_pos)[:, None, None, None] * (1.0 + 2.0 * depth_pos)[None, :, None, None])
    row_scale = jnp.exp(jax.random.uniform(key_rows, (NY,), jnp.float32, math.log(0.5), math.log(1.6)))
    col_scale = jnp.exp(jax.random.uniform(key_cols, (NX,), jnp.float32, math.log(0.5), math.log(1.6)))
    base = jax.random.truncated_normal(key_base, -5.0, 5.0, shape, jnp.float32)
    values = base * amplitude * row_scale[None, None, :, None] * col_scale[None, None, None, :]
    return values.astype(jnp.float32)


def steps_of(rng, extent, shards, low, largest):
    def one(dim, blocks):
        draws = jax.random.uniform(jax.random.fold_in(jax.random.fold_in(rng, 6), dim), (blocks,), jnp.float32, low / len(shards), largest / len(shards))
        return jnp.repeat(jnp.exp(draws), extent[dim] // blocks).reshape((-1,) + (1,) * (len(extent) - dim - 1))

    level = one(*shards[0])
    for cut in shards[1:]:
        level = level * one(*cut)
    return level


def setup_inputs(seed: int = 0) -> dict:
    splits = jax.random.split(jax.random.key(seed), 6)
    starts = draw_starts(jax.random.fold_in(splits[5], 71), 0)
    vel_x = jnp.clip(jax.random.uniform(splits[1], (NZ, NY, NX), jnp.float32, -0.15, 0.15) * steps_of(splits[1], (NZ, NY, NX), ((0, 16),), -0.4, 0.0), -0.15, 0.15)
    vel_y = jnp.clip(jax.random.uniform(splits[2], (NZ, NY, NX), jnp.float32, -0.15, 0.15) * steps_of(splits[2], (NZ, NY, NX), ((0, 16),), -0.4, 0.0), -0.15, 0.15)
    vel_z = jnp.clip(jax.random.uniform(splits[3], (NZ, NY, NX), jnp.float32, -0.5, 0.5) * steps_of(splits[3], (NZ, NY, NX), ((0, 16),), -0.4, 0.0), -0.5, 0.5)
    kappa = jnp.clip(jnp.exp(math.log(0.03) - 1.0986123 * jax.random.uniform(splits[4], (NZ, NY, NX), jnp.float32) ** steps_of(splits[4], (NZ, NY, NX), ((0, 16),), -0.2, 0.2)), 0.01, 0.03)
    return dict(starts=starts, vel_x=vel_x, vel_y=vel_y, vel_z=vel_z, kappa=kappa)


def advance(extended, vel_x, vel_y, vel_z, kappa):
    padded = jnp.pad(extended, ((0, 0), (1, 1), (1, 1)))
    center = padded[1:-1, 1:-1, 1:-1]
    z_minus = padded[:-2, 1:-1, 1:-1]
    z_plus = padded[2:, 1:-1, 1:-1]
    y_minus = padded[1:-1, :-2, 1:-1]
    y_plus = padded[1:-1, 2:, 1:-1]
    x_minus = padded[1:-1, 1:-1, :-2]
    x_plus = padded[1:-1, 1:-1, 2:]
    transport = jnp.maximum(vel_x, 0.0) * (center - x_minus) + jnp.minimum(vel_x, 0.0) * (x_plus - center)
    transport = transport + (jnp.maximum(vel_y, 0.0) * (center - y_minus) + jnp.minimum(vel_y, 0.0) * (y_plus - center))
    transport = transport + (jnp.maximum(vel_z, 0.0) * (center - z_minus) + jnp.minimum(vel_z, 0.0) * (z_plus - center))
    diffusion = kappa * (x_minus + x_plus + y_minus + y_plus + z_minus + z_plus - 6.0 * center)
    return center - transport + diffusion

def zpad(field):
    return jnp.pad(field, ((1, 1), (0, 0), (0, 0)))

def restrict(field):
    depth, rows, cols = field.shape
    return field.reshape(depth // 4, 4, rows // 4, 4, cols // 4, 4).mean(axis=(1, 3, 5))

def prolong(field):
    depth, rows, cols = field.shape
    wide = jnp.broadcast_to(field[:, None, :, None, :, None], (depth, 4, rows, 4, cols, 4))
    return wide.reshape(depth * 4, rows * 4, cols * 4)

def reference(starts, vel_x, vel_y, vel_z, kappa):
    courant_scale = FSTEPS / (4.0 * GC)
    diffusion_scale = FSTEPS / (16.0 * GC)
    coarse_x = restrict(vel_x) * courant_scale
    coarse_y = restrict(vel_y) * courant_scale
    coarse_z = restrict(vel_z) * courant_scale
    coarse_k = restrict(kappa) * diffusion_scale

    def fine(field):
        for step_index in range(FSTEPS):
            field = advance(zpad(field), vel_x, vel_y, vel_z, kappa)
        return field

    def coarse(field):
        for step_index in range(GC):
            field = advance(zpad(field), coarse_x, coarse_y, coarse_z, coarse_k)
        return field
    fine_ends = lax.map(fine, starts)
    coarse_now = restrict(starts[0])
    new_list = [starts[0]]
    for slice_index in range(SLICES - 1):
        fine_coarse = restrict(fine_ends[slice_index])
        drift_term = fine_coarse - coarse(restrict(starts[slice_index]))
        coarse_now = coarse(coarse_now) + drift_term
        new_list.append(fine_ends[slice_index] + prolong(coarse_now - fine_coarse))
    new_starts = jnp.stack(new_list)
    total_sum = jnp.sum((new_starts - starts) ** 2)
    change_norm = jnp.sqrt(total_sum / (SLICES * NZ * NY * NX) + 1e-06)
    return (new_starts, change_norm)
```

```python
import jax
import jax.numpy as jnp
from jax import lax
from jax.experimental import pallas as pl
from jax.experimental.pallas import tpu as pltpu
from jax.sharding import PartitionSpec as P


FSTEPS = 6
GC = 2
NZL, NY, NX = 12, 64, 128
SL = 16
SP = 16
NCELL = SL * 192 * NY * NX
COURANT = FSTEPS / (4.0 * GC)
DIFFUSE = FSTEPS / (16.0 * GC)

F32 = jnp.float32
ANY = pl.BlockSpec(memory_space=pl.ANY)
VM = pl.BlockSpec(memory_space=pltpu.VMEM)


def near(x):
    return pltpu.with_memory_space_constraint(x, pltpu.VMEM)


def run_all(copies):
    for c in copies:
        c.start()
    for c in copies:
        c.wait()


def pack_kernel(st, vx, vy, vz, ka, pa, pb, sem):
    core = lax.rem(lax.axis_index("tm"), 2)
    odd = lax.rem(lax.axis_index("space"), 2)
    au, ac = 6 * (1 - odd), 7 * (1 - odd)
    bu, bc = 6 * odd, 7 * odd

    def go(f0, f1):
        pairs = [
            (st.at[0, pl.ds(au, 6)], pa.at[0:6]),
            (f0.at[pl.ds(ac, 5)], pa.at[6:11]),
            (f1.at[pl.ds(ac, 5)], pa.at[11:16]),
            (st.at[0, pl.ds(bu, 6)], pb.at[0:6]),
            (f0.at[pl.ds(bc, 5)], pb.at[6:11]),
            (f1.at[pl.ds(bc, 5)], pb.at[11:16]),
        ]
        run_all([pltpu.make_async_copy(a, b, sem.at[i]) for i, (a, b) in enumerate(pairs)])

    @pl.when(core == 0)
    def _():
        go(vx, vy)

    @pl.when(core == 1)
    def _():
        go(vz, ka)


def block_sum(v):
    row = lax.broadcasted_iota(jnp.int32, v.shape, 1)
    lane = lax.broadcasted_iota(jnp.int32, v.shape, 2)
    v = v + jnp.where((row & 1) == 0, pltpu.roll(v, 7, 1), pltpu.roll(v, 1, 1))
    v = v + jnp.where((row & 2) == 0, pltpu.roll(v, 6, 1), pltpu.roll(v, 2, 1))
    v = v + jnp.where((lane & 1) == 0, pltpu.roll(v, 127, 2), pltpu.roll(v, 1, 2))
    v = v + jnp.where((lane & 2) == 0, pltpu.roll(v, 126, 2), pltpu.roll(v, 2, 2))
    return v


def fine_kernel(st, nx, vx, vy, vz, ka, ra, rb, sa, sb, fine, pay, u, c, w, rows, ck, sem):
    n = lax.axis_index("tm")
    s = lax.axis_index("space")
    core = lax.rem(n, 2)
    odd = lax.rem(s, 2)
    au, ac = 18 * (1 - odd), 17 * (1 - odd)
    bu, bc = 18 * odd, 17 * odd
    own = 2 * core
    oth = 2 - own
    pairs = [
        (vx, c.at[0, 5:17]),
        (vy, c.at[1, 5:17]),
        (vz, c.at[2, 5:17]),
        (ka, c.at[3, 5:17]),
        (ra.at[6:11], c.at[own, pl.ds(ac, 5)]),
        (ra.at[11:16], c.at[own + 1, pl.ds(ac, 5)]),
        (rb.at[6:11], c.at[own, pl.ds(bc, 5)]),
        (rb.at[11:16], c.at[own + 1, pl.ds(bc, 5)]),
        (sa.at[6:11], c.at[oth, pl.ds(ac, 5)]),
        (sa.at[11:16], c.at[oth + 1, pl.ds(ac, 5)]),
        (sb.at[6:11], c.at[oth, pl.ds(bc, 5)]),
        (sb.at[11:16], c.at[oth + 1, pl.ds(bc, 5)]),
        (st.at[0], u.at[0, 6:18]),
        (ra.at[0:6], u.at[0, pl.ds(au, 6)]),
        (rb.at[0:6], u.at[0, pl.ds(bu, 6)]),
    ]
    run_all([pltpu.make_async_copy(a, b, sem.at[i]) for i, (a, b) in enumerate(pairs)])

    row = lax.broadcasted_iota(jnp.int32, (NY, NX), 0)
    lane = lax.broadcasted_iota(jnp.int32, (NY, NX), 1)

    def weights(i, _):
        k = c[3, i]
        cx, cy, cz = c[0, i], c[1, i], c[2, i]
        xm, xp = k + jnp.maximum(cx, 0.0), k - jnp.minimum(cx, 0.0)
        ym, yp = k + jnp.maximum(cy, 0.0), k - jnp.minimum(cy, 0.0)
        zm, zp = k + jnp.maximum(cz, 0.0), k - jnp.minimum(cz, 0.0)
        w[0, i] = 1.0 - ((xm + xp) + (ym + yp) + (zm + zp))
        w[1, i] = jnp.where(lane == 0, 0.0, xm)
        w[2, i] = jnp.where(lane == NX - 1, 0.0, xp)
        w[3, i] = jnp.where(row == 0, 0.0, ym)
        w[4, i] = jnp.where(row == NY - 1, 0.0, yp)
        w[5, i] = zm
        w[6, i] = zp
        return 0

    lax.fori_loop(0, 22, weights, 0)

    for t in range(FSTEPS):
        a, b = t % 2, (t + 1) % 2

        def plane(p, _, a=a, b=b, last=t == FSTEPS - 1):
            v = u[a, p]
            i = p - 1
            x = w[1, i] * pltpu.roll(v, 1, 1) + w[2, i] * pltpu.roll(v, NX - 1, 1)
            y = w[3, i] * pltpu.roll(v, 1, 0) + w[4, i] * pltpu.roll(v, NY - 1, 0)
            z = w[5, i] * u[a, p - 1] + w[6, i] * u[a, p + 1]
            new = w[0, i] * v + (x + (y + z))
            if last:
                fine[p - 6] = new
            else:
                u[b, p] = new
            return 0

        lax.fori_loop(1 + t, 23 - t, plane, 0, unroll=2)


    lane8 = lax.broadcasted_iota(jnp.int32, (8, NX), 1)
    live = jnp.where(n < SL - 1, 1.0, 0.0).astype(F32)
    f = n // 4
    scale = jnp.where(f < 3, COURANT / 64.0, DIFFUSE / 64.0).astype(F32)
    var = jnp.zeros((8, NX), F32)

    def pack(m, base):
        for h in range(2):
            d = jnp.zeros((8, NX), F32)
            for q in range(4):
                d = d + jnp.where((lane8 & 3) == q, m[2 * q + h], 0.0)
            rows[base + 8 * h : base + 8 * h + 8, :] = d

    for zl in range(3):
        ds = [
            (fine[4 * zl + i] - nx[4 * zl + i]).reshape(8, 8, NX) for i in range(4)
        ]
        m = block_sum((ds[0] + ds[1]) + (ds[2] + ds[3])) * (1.0 / 64.0)
        for d in ds:
            r = d - m
            var = var + jnp.sum(r * r, axis=0)
        pack(m, 16 * zl)
        cs = [c[f, 5 + 4 * zl + i].reshape(8, 8, NX) for i in range(4)]
        pack(block_sum((cs[0] + cs[1]) + (cs[2] + cs[3])) * scale, 48 + 16 * zl)

    src = lax.broadcasted_iota(jnp.int32, (NX, NX), 0)
    dst = lax.broadcasted_iota(jnp.int32, (NX, NX), 1)
    perm = jnp.where(src == 4 * (dst & 31) + (dst >> 5), 1.0, 0.0).astype(F32)
    ck[...] = jnp.dot(rows[...], perm, precision=lax.Precision.HIGHEST, preferred_element_type=F32)
    for r in range(4):
        for zl in range(3):
            pay[0, r * 3 + zl : r * 3 + zl + 1, :] = ck[16 * zl + 4 * r : 16 * zl + 4 * r + 1, :]
    rr = lax.rem(n, 4)
    for zl in range(3):
        pay[0, 12 + zl : 13 + zl, :] = ck[pl.ds(48 + 16 * zl + 4 * rr, 1), :]
    pay[0, 15:16, :] = jnp.sum(var, axis=0, keepdims=True) * live
    for z in range(1, 8):
        pay[z] = pay[0]


def sweep_kernel(ga, gb, fine, st, out, change, jj, w, gs, base, sem):
    nd = lax.axis_index("tm")
    s = lax.axis_index("space")
    core = lax.rem(nd, 2)

    @pl.when(core == 0)
    def _():
        run_all([pltpu.make_async_copy(ga, jj.at[0], sem.at[0]), pltpu.make_async_copy(gb, jj.at[1], sem.at[1])])

    @pl.when(core == 1)
    def _():
        run_all([pltpu.make_async_copy(ga, jj.at[1], sem.at[0]), pltpu.make_async_copy(gb, jj.at[0], sem.at[1])])

    @pl.when(nd == 0)
    def _():
        run_all([pltpu.make_async_copy(st.at[0], base, sem.at[2])])

    @pl.when(nd > 0)
    def _():
        run_all([pltpu.make_async_copy(fine, base, sem.at[2])])

    def load(n, q, h):
        start = h * 1024 + (n // 2) * 16 + q
        return jj[lax.rem(n, 2), pl.ds(start, 8, stride=128), :]

    row = lax.broadcasted_iota(jnp.int32, (8, NX), 0)
    lane = lax.broadcasted_iota(jnp.int32, (8, NX), 1)
    x_lo, x_hi = (lane & 31) == 0, (lane & 31) == 31
    y_lo, y_hi = lane < 32, lane >= 96
    z_lo, z_hi = row == 0, row == 7

    def at(r, zl, h):
        return (r * 3 + zl) * 2 + h

    cells = [(r, zl, h) for r in range(4) for zl in range(3) for h in range(2)]
    for r, zl, h in cells:
        cx, cy, cz, k = (load(4 * f + r, 12 + zl, h) for f in range(4))
        xm, xp = k + jnp.maximum(cx, 0.0), k - jnp.minimum(cx, 0.0)
        ym, yp = k + jnp.maximum(cy, 0.0), k - jnp.minimum(cy, 0.0)
        zm, zp = k + jnp.maximum(cz, 0.0), k - jnp.minimum(cz, 0.0)
        i = at(r, zl, h)
        w[0, i] = 1.0 - ((xm + xp) + (ym + yp) + (zm + zp))
        w[1, i] = jnp.where(x_lo, 0.0, xm)
        w[2, i] = jnp.where(x_hi, 0.0, xp)
        w[3, i] = jnp.where(y_lo, 0.0, ym) if r == 0 else ym
        w[4, i] = jnp.where(y_hi, 0.0, yp) if r == 3 else yp
        w[5, i] = jnp.where(z_lo, 0.0, zm) if zl == 0 and h == 0 else zm
        w[6, i] = jnp.where(z_hi, 0.0, zp) if zl == 2 and h == 1 else zp

    def coarse_step(e):
        new = []
        low = {}
        high = {}
        for r in range(4):
            dn = [pltpu.roll(e[at(r, 2, h)], 1, 0) for h in range(2)]
            low[r] = [dn[0], jnp.where(z_lo, dn[0], dn[1])]
            up = [pltpu.roll(e[at(r, 0, h)], 7, 0) for h in range(2)]
            high[r] = [jnp.where(z_hi, up[1], up[0]), up[1]]
        for r, zl, h in cells:
            i = at(r, zl, h)
            v = e[i]
            y0 = e[at(r - 1, zl, h)] if r > 0 else pltpu.roll(e[at(3, zl, h)], 32, 1)
            y1 = e[at(r + 1, zl, h)] if r < 3 else pltpu.roll(e[at(0, zl, h)], 96, 1)
            z0 = e[at(r, zl - 1, h)] if zl > 0 else low[r][h]
            z1 = e[at(r, zl + 1, h)] if zl < 2 else high[r][h]
            x = w[1, i] * pltpu.roll(v, 1, 1) + w[2, i] * pltpu.roll(v, NX - 1, 1)
            y = w[3, i] * y0 + w[4, i] * y1
            z = w[5, i] * z0 + w[6, i] * z1
            new.append(w[0, i] * v + (x + (y + z)))
        return tuple(new)

    zero = jnp.zeros((8, NX), F32)
    e = tuple(load(0, r * 3 + zl, h) for r, zl, h in cells)
    acc = zero
    for v in e:
        acc = acc + v * v
    for q in range(12):
        gs[0, q] = jnp.zeros((16, NX), F32)

    def turn(n, carry):
        e, acc = carry
        for _ in range(GC):
            e = coarse_step(e)
        new = []
        for r, zl, h in cells:
            g = e[at(r, zl, h)]
            gs[n, r * 3 + zl, 8 * h : 8 * h + 8, :] = g
            v = g + load(n, r * 3 + zl, h)
            acc = acc + v * v
            new.append(v)
        return tuple(new), acc

    e, acc = lax.fori_loop(1, SL - 1, turn, (e, acc))

    part = zero
    for cc in range(2):
        for b in range(16):
            part = part + jj[cc, pl.ds(b * 128 + 15, 8, stride=16), :]
    total = jnp.sum(part + 64.0 * acc)
    value = jnp.sqrt(jnp.full((8, NX), total / NCELL, F32) + 1e-06)
    change[0, 0] = jnp.max(value)

    prev = jnp.maximum(nd - 1, 0)
    g12 = jnp.concatenate([gs[prev, q, pl.ds(s, 1), :] for q in range(12)] + [jnp.zeros((4, NX), F32)], axis=0)
    src = lax.broadcasted_iota(jnp.int32, (NX, 4 * NX), 0)
    dst = lax.broadcasted_iota(jnp.int32, (NX, 4 * NX), 1)
    spread = jnp.where(src == 32 * (dst >> 7) + ((dst & 127) >> 2), 1.0, 0.0).astype(F32)
    wide = jnp.dot(g12, spread, precision=lax.Precision.HIGHEST, preferred_element_type=F32)

    for zl in range(3):
        for q in range(4):
            for h in range(2):
                lo = wide[2 * h * 3 + zl : 2 * h * 3 + zl + 1, q * NX : (q + 1) * NX]
                hi = wide[(2 * h + 1) * 3 + zl : (2 * h + 1) * 3 + zl + 1, q * NX : (q + 1) * NX]
                tile = jnp.where(row < 4, jnp.broadcast_to(lo, (8, NX)), jnp.broadcast_to(hi, (8, NX)))
                y = 8 * (2 * q + h)
                for i in range(4):
                    out[0, 4 * zl + i, y : y + 8, :] = base[4 * zl + i, y : y + 8, :] + tile


def per_device(starts, vel_x, vel_y, vel_z, kappa):
    plane = (NY, NX)
    shape = jax.ShapeDtypeStruct
    even = [(i, i ^ 1) for i in range(SP)]
    odd = [(i, i + 1) for i in range(1, SP - 1, 2)] + [(i + 1, i) for i in range(1, SP - 1, 2)]
    swap = [(i, i ^ 1) for i in range(SL)]
    down = [(i + 1, i) for i in range(SL - 1)]
    up = [(i, i + 1) for i in range(SL - 1)]
    zgroups = [[c + 2 * z for z in range(8)] for c in range(2)]

    pay_a, pay_b = pl.pallas_call(
        pack_kernel,
        out_shape=(pltpu.VMEM((16,) + plane, F32),) * 2,
        in_specs=[ANY] * 5,
        out_specs=(VM, VM),
        scratch_shapes=[pltpu.SemaphoreType.DMA((6,))],
        name="pack",
    )(starts, vel_x, vel_y, vel_z, kappa)
    nxt = lax.ppermute(starts[0], "tm", down)
    ra = lax.ppermute(pay_a, "space", even)
    rb = lax.ppermute(pay_b, "space", odd)
    sa = lax.ppermute(ra, "tm", swap)
    sb = lax.ppermute(rb, "tm", swap)

    fine, pay = pl.pallas_call(
        fine_kernel,
        out_shape=(pltpu.VMEM((NZL,) + plane, F32), pltpu.VMEM((8, 16, NX), F32)),
        in_specs=[ANY, VM] + [ANY] * 4 + [VM] * 4,
        out_specs=(VM, VM),
        scratch_shapes=[
            pltpu.VMEM((2, 24) + plane, F32),
            pltpu.VMEM((4, 22) + plane, F32),
            pltpu.VMEM((7, 22) + plane, F32),
            pltpu.VMEM((96, NX), F32),
            pltpu.VMEM((96, NX), F32),
            pltpu.SemaphoreType.DMA((15,)),
        ],
        name="fine",
    )(starts, near(nxt), vel_x, vel_y, vel_z, kappa, near(ra), near(rb), near(sa), near(sb))

    gz = lax.all_to_all(pay, "tm", 0, 0, axis_index_groups=zgroups)
    fine, gz = lax.optimization_barrier((fine, gz))
    moved = lax.ppermute(fine, "tm", up)
    ga = lax.all_to_all(jnp.broadcast_to(gz[None], (16, 8, 16, NX)), "space", 0, 0)
    gb = lax.ppermute(ga, "tm", swap)

    new, change = pl.pallas_call(
        sweep_kernel,
        out_shape=(shape((1, NZL) + plane, F32), shape((1, 1), F32)),
        in_specs=[VM, VM, VM, ANY],
        out_specs=(VM, pl.BlockSpec(memory_space=pltpu.SMEM)),
        scratch_shapes=[
            pltpu.VMEM((2, 2048, NX), F32),
            pltpu.VMEM((7, 24, 8, NX), F32),
            pltpu.VMEM((15, 12, 16, NX), F32),
            pltpu.VMEM((12,) + plane, F32),
            pltpu.SemaphoreType.DMA((3,)),
        ],
        name="sweep",
    )(near(ga.reshape(2048, NX)), near(gb.reshape(2048, NX)), near(moved), starts)
    return new, change.reshape(())


def solution(mesh):
    return jax.shard_map(
        per_device,
        mesh=mesh,
        in_specs=(
            P("tm", "space", None, None),
            P("space", None, None),
            P("space", None, None),
            P("space", None, None),
            P("space", None, None),
        ),
        out_specs=(P("tm", "space", None, None), P()),
        check_vma=False,
    )
```

```python
import jax
import jax.numpy as jnp
from jax import lax
from jax.experimental import pallas as pl
from jax.experimental.pallas import tpu as pltpu
from jax.sharding import PartitionSpec as P


FSTEPS = 6
GC = 2
NZL, NY, NX = 12, 64, 128
SL = 16
SP = 16
NCELL = SL * 192 * NY * NX
COURANT = FSTEPS / (4.0 * GC)
DIFFUSE = FSTEPS / (16.0 * GC)

F32 = jnp.float32
LIMIT = 24 << 20
HBM = pl.BlockSpec(memory_space=pltpu.HBM)
VM = pl.BlockSpec(memory_space=pltpu.VMEM)


def near(x):
    return pltpu.with_memory_space_constraint(x, pltpu.VMEM)


def far(x):
    return pltpu.with_memory_space_constraint(x, pltpu.HBM)


def run_all(copies):
    for c in copies:
        c.start()
    for c in copies:
        c.wait()


def pack_kernel(st, vx, vy, vz, ka, pa, pb, sem):
    core = lax.rem(lax.axis_index("tm"), 2)
    odd = lax.rem(lax.axis_index("space"), 2)
    au, ac = 6 * (1 - odd), 7 * (1 - odd)
    bu, bc = 6 * odd, 7 * odd

    def go(f0, f1):
        pairs = [
            (st.at[0, pl.ds(au, 6)], pa.at[0:6]),
            (f0.at[pl.ds(ac, 5)], pa.at[6:11]),
            (f1.at[pl.ds(ac, 5)], pa.at[11:16]),
            (st.at[0, pl.ds(bu, 6)], pb.at[0:6]),
            (f0.at[pl.ds(bc, 5)], pb.at[6:11]),
            (f1.at[pl.ds(bc, 5)], pb.at[11:16]),
        ]
        run_all([pltpu.make_async_copy(a, b, sem.at[i]) for i, (a, b) in enumerate(pairs)])

    @pl.when(core == 0)
    def _():
        go(vx, vy)

    @pl.when(core == 1)
    def _():
        go(vz, ka)


def block_sum(v):
    row = lax.broadcasted_iota(jnp.int32, v.shape, 1)
    lane = lax.broadcasted_iota(jnp.int32, v.shape, 2)
    v = v + jnp.where((row & 1) == 0, pltpu.roll(v, 7, 1), pltpu.roll(v, 1, 1))
    v = v + jnp.where((row & 2) == 0, pltpu.roll(v, 6, 1), pltpu.roll(v, 2, 1))
    v = v + jnp.where((lane & 1) == 0, pltpu.roll(v, 127, 2), pltpu.roll(v, 1, 2))
    v = v + jnp.where((lane & 2) == 0, pltpu.roll(v, 126, 2), pltpu.roll(v, 2, 2))
    return v


def coarse_rows(m, rows, base):
    lane = lax.broadcasted_iota(jnp.int32, (8, NX), 1)
    for h in range(2):
        d = jnp.zeros((8, NX), F32)
        for q in range(4):
            d = d + jnp.where((lane & 3) == q, m[2 * q + h], 0.0)
        rows[base + 8 * h : base + 8 * h + 8, :] = d


def spread_lanes(rows):
    src = lax.broadcasted_iota(jnp.int32, (NX, NX), 0)
    dst = lax.broadcasted_iota(jnp.int32, (NX, NX), 1)
    perm = jnp.where(src == 4 * (dst & 31) + (dst >> 5), 1.0, 0.0).astype(F32)
    return jnp.dot(rows, perm, precision=lax.Precision.HIGHEST, preferred_element_type=F32)


def mix(v, before, after, w, i):
    x = w[1, i] * pltpu.roll(v, 1, 1) + w[2, i] * pltpu.roll(v, NX - 1, 1)
    y = w[3, i] * pltpu.roll(v, 1, 0) + w[4, i] * pltpu.roll(v, NY - 1, 0)
    z = w[5, i] * before + w[6, i] * after
    return w[0, i] * v + (x + (y + z))


def put_weights(w, i, cx, cy, cz, k):
    row = lax.broadcasted_iota(jnp.int32, (NY, NX), 0)
    lane = lax.broadcasted_iota(jnp.int32, (NY, NX), 1)
    xm, xp = k + jnp.maximum(cx, 0.0), k - jnp.minimum(cx, 0.0)
    ym, yp = k + jnp.maximum(cy, 0.0), k - jnp.minimum(cy, 0.0)
    zm, zp = k + jnp.maximum(cz, 0.0), k - jnp.minimum(cz, 0.0)
    w[0, i] = 1.0 - ((xm + xp) + (ym + yp) + (zm + zp))
    w[1, i] = jnp.where(lane == 0, 0.0, xm)
    w[2, i] = jnp.where(lane == NX - 1, 0.0, xp)
    w[3, i] = jnp.where(row == 0, 0.0, ym)
    w[4, i] = jnp.where(row == NY - 1, 0.0, yp)
    w[5, i] = zm
    w[6, i] = zp


def prep_kernel(st, vx, vy, vz, ka, w, lev, part, c, rows, ck, sem):
    n = lax.axis_index("tm")
    pairs = [(vx, c.at[0]), (vy, c.at[1]), (vz, c.at[2]), (ka, c.at[3]), (st.at[0], lev.at[0])]
    run_all([pltpu.make_async_copy(a, b, sem.at[i]) for i, (a, b) in enumerate(pairs)])

    def weights(i, _):
        put_weights(w, i, c[0, i], c[1, i], c[2, i], c[3, i])
        return 0

    lax.fori_loop(0, NZL, weights, 0)

    for t in range(1, FSTEPS):

        def plane(q, _, t=t):
            lev[t, q] = mix(lev[t - 1, q], lev[t - 1, q - 1], lev[t - 1, q + 1], w, q)
            return 0

        lax.fori_loop(t, NZL - t, plane, 0, unroll=2)

    f = n // 4
    scale = jnp.where(f < 3, COURANT / 64.0, DIFFUSE / 64.0).astype(F32)
    for zl in range(3):
        cs = [c[f, 4 * zl + i].reshape(8, 8, NX) for i in range(4)]
        coarse_rows(block_sum((cs[0] + cs[1]) + (cs[2] + cs[3])) * scale, rows, 16 * zl)
    ck[...] = spread_lanes(rows[...])
    for zl in range(3):
        part[zl : zl + 1, :] = ck[pl.ds(16 * zl + 4 * lax.rem(n, 4), 1), :]


def wedge(hi, own, other, w, lev, put, u, wk):
    first = lax.rem(lax.axis_index("tm"), 2) == 0
    sign = (1 - 2 * hi).astype(F32)

    def slab(k):
        return (k - 6) + hi * (23 - 2 * k)

    def halo(k, _):
        j = (k - 1) + hi * (6 - 2 * k)
        a0, a1, b0, b1 = own[6 + j], own[11 + j], other[6 + j], other[11 + j]
        put_weights(
            wk,
            k,
            jnp.where(first, a0, b0),
            jnp.where(first, a1, b1),
            jnp.where(first, b0, a0) * sign,
            jnp.where(first, b1, a1),
        )
        return 0

    def center(k, _):
        q = slab(k)
        for i in range(5):
            wk[i, k] = w[i, q]
        wk[5, k] = w[5 + hi, q]
        wk[6, k] = w[6 - hi, q]
        return 0

    lax.fori_loop(1, 6, halo, 0)
    lax.fori_loop(6, 12, center, 0)
    for k in range(6):
        u[0, k] = own[k + hi * (5 - 2 * k)]

    for t in range(1, FSTEPS + 1):
        a, b = (t - 1) % 2, t % 2
        for k in (5 + t, 6 + t):
            u[a, k] = lev[t - 1, slab(k)]

        def plane(k, _, a=a, b=b, t=t):
            new = mix(u[a, k], u[a, k - 1], u[a, k + 1], wk, k)
            if t == FSTEPS:
                put(k, slab(k), new)
            else:
                u[b, k] = new
            return 0

        lax.fori_loop(t, t + 6, plane, 0, unroll=2)
    return slab


def first_kernel(own, other, w, lev, half, u, wk):
    def put(k, q, new):
        half[k - 6] = new

    wedge(1 - lax.rem(lax.axis_index("space"), 2), own, other, w, lev, put, u, wk)


def second_kernel(own, other, w, lev, half, part, nx, fine, pay, u, wk, rows, ck):
    n = lax.axis_index("tm")
    hi = lax.rem(lax.axis_index("space"), 2)

    def put(k, q, new):
        fine[q] = new

    wedge(hi, own, other, w, lev, put, u, wk)
    for i in range(6):
        fine[i * (2 * hi - 1) + 11 * (1 - hi)] = half[i]

    live = jnp.where(n < SL - 1, 1.0, 0.0).astype(F32)
    var = jnp.zeros((8, NX), F32)
    for zl in range(3):
        ds = [(fine[4 * zl + i] - nx[4 * zl + i]).reshape(8, 8, NX) for i in range(4)]
        m = block_sum((ds[0] + ds[1]) + (ds[2] + ds[3])) * (1.0 / 64.0)
        for d in ds:
            r = d - m
            var = var + jnp.sum(r * r, axis=0)
        coarse_rows(m, rows, 16 * zl)
    ck[...] = spread_lanes(rows[...])
    for r in range(4):
        for zl in range(3):
            pay[0, r * 3 + zl : r * 3 + zl + 1, :] = ck[16 * zl + 4 * r : 16 * zl + 4 * r + 1, :]
    pay[0, 12:15, :] = part[0:3, :]
    pay[0, 15:16, :] = jnp.sum(var, axis=0, keepdims=True) * live
    for z in range(1, 8):
        pay[z] = pay[0]


def sweep_kernel(ga, gb, fine, st, out, change, w, gs, accs, sem):
    core = lax.rem(lax.axis_index("tm"), 2)

    @pl.when(core == 0)
    def _():
        sweep(ga, gb, w, gs, accs)

    @pl.when(core == 1)
    def _():
        sweep(gb, ga, w, gs, accs)

    finish(fine, st, out, change, gs, accs, sem)


def sweep(even, odd, w, gs, accs):
    def load(ref, z, q, h):
        return ref[pl.ds(h * 1024 + z * 16 + q, 8, stride=128), :]

    row = lax.broadcasted_iota(jnp.int32, (8, NX), 0)
    lane = lax.broadcasted_iota(jnp.int32, (8, NX), 1)
    x_lo, x_hi = (lane & 31) == 0, (lane & 31) == 31
    y_lo, y_hi = lane < 32, lane >= 96
    z_lo, z_hi = row == 0, row == 7

    def at(r, zl, h):
        return (r * 3 + zl) * 2 + h

    cells = [(r, zl, h) for r in range(4) for zl in range(3) for h in range(2)]
    for r, zl, h in cells:
        cx, cy, cz, k = (load((even, odd)[r % 2], 2 * f + r // 2, 12 + zl, h) for f in range(4))
        xm, xp = k + jnp.maximum(cx, 0.0), k - jnp.minimum(cx, 0.0)
        ym, yp = k + jnp.maximum(cy, 0.0), k - jnp.minimum(cy, 0.0)
        zm, zp = k + jnp.maximum(cz, 0.0), k - jnp.minimum(cz, 0.0)
        i = at(r, zl, h)
        w[0, i] = 1.0 - ((xm + xp) + (ym + yp) + (zm + zp))
        w[1, i] = jnp.where(x_lo, 0.0, xm)
        w[2, i] = jnp.where(x_hi, 0.0, xp)
        w[3, i] = jnp.where(y_lo, 0.0, ym) if r == 0 else ym
        w[4, i] = jnp.where(y_hi, 0.0, yp) if r == 3 else yp
        w[5, i] = jnp.where(z_lo, 0.0, zm) if zl == 0 and h == 0 else zm
        w[6, i] = jnp.where(z_hi, 0.0, zp) if zl == 2 and h == 1 else zp

    def coarse_step(e):
        new = []
        low = {}
        high = {}
        for r in range(4):
            dn = [pltpu.roll(e[at(r, 2, h)], 1, 0) for h in range(2)]
            low[r] = [dn[0], jnp.where(z_lo, dn[0], dn[1])]
            up = [pltpu.roll(e[at(r, 0, h)], 7, 0) for h in range(2)]
            high[r] = [jnp.where(z_hi, up[1], up[0]), up[1]]
        for r, zl, h in cells:
            i = at(r, zl, h)
            v = e[i]
            y0 = e[at(r - 1, zl, h)] if r > 0 else pltpu.roll(e[at(3, zl, h)], 32, 1)
            y1 = e[at(r + 1, zl, h)] if r < 3 else pltpu.roll(e[at(0, zl, h)], 96, 1)
            z0 = e[at(r, zl - 1, h)] if zl > 0 else low[r][h]
            z1 = e[at(r, zl + 1, h)] if zl < 2 else high[r][h]
            x = w[1, i] * pltpu.roll(v, 1, 1) + w[2, i] * pltpu.roll(v, NX - 1, 1)
            y = w[3, i] * y0 + w[4, i] * y1
            z = w[5, i] * z0 + w[6, i] * z1
            new.append(w[0, i] * v + (x + (y + z)))
        return tuple(new)

    e = tuple(load(even, 0, r * 3 + zl, h) for r, zl, h in cells)
    acc = jnp.zeros((8, NX), F32)
    for v in e:
        acc = acc + v * v
    for q in range(12):
        gs[0, q] = jnp.zeros((16, NX), F32)

    def turn(ref, z, n, e, acc):
        for _ in range(GC):
            e = coarse_step(e)
        new = []
        for r, zl, h in cells:
            g = e[at(r, zl, h)]
            gs[n, r * 3 + zl, 8 * h : 8 * h + 8, :] = g
            v = g + load(ref, z, r * 3 + zl, h)
            acc = acc + v * v
            new.append(v)
        return tuple(new), acc

    def two(z, carry):
        e, acc = turn(odd, z, 2 * z + 1, *carry)
        return turn(even, z + 1, 2 * z + 2, e, acc)

    e, acc = lax.fori_loop(0, 7, two, (e, acc))

    part = jnp.zeros((8, NX), F32)
    for ref in (even, odd):
        for b in range(16):
            part = part + ref[pl.ds(b * 128 + 15, 8, stride=16), :]
    accs[...] = part + 64.0 * acc


def finish(fine, st, out, change, gs, accs, sem):
    nd = lax.axis_index("tm")
    s = lax.axis_index("space")
    row = lax.broadcasted_iota(jnp.int32, (8, NX), 0)
    value = jnp.sqrt(jnp.full((8, NX), jnp.sum(accs[...]) / NCELL, F32) + 1e-06)
    change[0, 0] = jnp.max(value)

    prev = jnp.maximum(nd - 1, 0)
    g12 = jnp.concatenate([gs[prev, q, pl.ds(s, 1), :] for q in range(12)] + [jnp.zeros((4, NX), F32)], axis=0)
    src = lax.broadcasted_iota(jnp.int32, (NX, 4 * NX), 0)
    dst = lax.broadcasted_iota(jnp.int32, (NX, 4 * NX), 1)
    spread = jnp.where(src == 32 * (dst >> 7) + ((dst & 127) >> 2), 1.0, 0.0).astype(F32)
    wide = jnp.dot(g12, spread, precision=lax.Precision.HIGHEST, preferred_element_type=F32)

    @pl.when(nd == 0)
    def _():
        run_all([pltpu.make_async_copy(st.at[0], out.at[0], sem.at[0])])

    @pl.when(nd > 0)
    def _():
        for zl in range(3):
            for q in range(4):
                for h in range(2):
                    i0, i1 = 6 * h + zl, 6 * h + 3 + zl
                    lo = wide[i0 : i0 + 1, q * NX : (q + 1) * NX]
                    hi = wide[i1 : i1 + 1, q * NX : (q + 1) * NX]
                    tile = jnp.where(row < 4, jnp.broadcast_to(lo, (8, NX)), jnp.broadcast_to(hi, (8, NX)))
                    y = 8 * (2 * q + h)
                    for i in range(4):
                        out[0, 4 * zl + i, y : y + 8, :] = fine[4 * zl + i, y : y + 8, :] + tile


def per_device(starts, vel_x, vel_y, vel_z, kappa):
    plane = (NY, NX)
    shape = jax.ShapeDtypeStruct
    even = [(i, i ^ 1) for i in range(SP)]
    odd = [(i, i + 1) for i in range(1, SP - 1, 2)] + [(i + 1, i) for i in range(1, SP - 1, 2)]
    swap = [(i, i ^ 1) for i in range(SL)]
    down = [(i + 1, i) for i in range(SL - 1)]
    up = [(i, i + 1) for i in range(SL - 1)]
    zgroups = [[c + 2 * z for z in range(8)] for c in range(2)]

    pay_a, pay_b = pl.pallas_call(
        pack_kernel,
        out_shape=(pltpu.VMEM((16,) + plane, F32),) * 2,
        in_specs=[HBM] * 5,
        out_specs=(VM, VM),
        scratch_shapes=[pltpu.SemaphoreType.DMA((6,))],
        compiler_params=pltpu.CompilerParams(vmem_limit_bytes=LIMIT),
        name="pack",
    )(*(far(x) for x in (starts, vel_x, vel_y, vel_z, kappa)))
    rb = lax.ppermute(pay_b, "space", odd)
    ra = lax.ppermute(pay_a, "space", even)
    nxt = lax.ppermute(starts[0], "tm", down)
    w, lev, part = pl.pallas_call(
        prep_kernel,
        out_shape=(
            pltpu.VMEM((7, NZL) + plane, F32),
            pltpu.VMEM((FSTEPS, NZL) + plane, F32),
            pltpu.VMEM((8, NX), F32),
        ),
        in_specs=[HBM] * 5,
        out_specs=(VM, VM, VM),
        scratch_shapes=[
            pltpu.VMEM((4, NZL) + plane, F32),
            pltpu.VMEM((48, NX), F32),
            pltpu.VMEM((48, NX), F32),
            pltpu.SemaphoreType.DMA((5,)),
        ],
        compiler_params=pltpu.CompilerParams(vmem_limit_bytes=LIMIT),
        name="prep",
    )(*(far(x) for x in (starts, vel_x, vel_y, vel_z, kappa)))
    work = [pltpu.VMEM((2, 13) + plane, F32), pltpu.VMEM((7, 12) + plane, F32)]
    sa = lax.ppermute(ra, "tm", swap)
    half = pl.pallas_call(
        first_kernel,
        out_shape=pltpu.VMEM((6,) + plane, F32),
        in_specs=[VM] * 4,
        out_specs=VM,
        scratch_shapes=work,
        compiler_params=pltpu.CompilerParams(vmem_limit_bytes=LIMIT),
        name="first",
    )(near(ra), near(sa), near(w), near(lev))
    sb = lax.ppermute(rb, "tm", swap)
    fine, pay = pl.pallas_call(
        second_kernel,
        out_shape=(pltpu.VMEM((NZL,) + plane, F32), pltpu.VMEM((8, 16, NX), F32)),
        in_specs=[VM] * 7,
        out_specs=(VM, VM),
        scratch_shapes=work + [pltpu.VMEM((48, NX), F32), pltpu.VMEM((48, NX), F32)],
        compiler_params=pltpu.CompilerParams(vmem_limit_bytes=LIMIT),
        name="second",
    )(near(rb), near(sb), near(w), near(lev), near(half), near(part), near(nxt))

    gz = lax.all_to_all(pay, "tm", 0, 0, axis_index_groups=zgroups)
    fine, gz = lax.optimization_barrier((fine, gz))
    moved = lax.ppermute(fine, "tm", up)
    ga = lax.all_to_all(jnp.broadcast_to(gz[None], (16, 8, 16, NX)), "space", 0, 0)
    gb = lax.ppermute(ga, "tm", swap)

    new, change = pl.pallas_call(
        sweep_kernel,
        out_shape=(shape((1, NZL) + plane, F32), shape((1, 1), F32)),
        in_specs=[VM, VM, VM, HBM],
        out_specs=(VM, pl.BlockSpec(memory_space=pltpu.SMEM)),
        scratch_shapes=[
            pltpu.VMEM((7, 24, 8, NX), F32),
            pltpu.VMEM((15, 12, 16, NX), F32),
            pltpu.VMEM((8, NX), F32),
            pltpu.SemaphoreType.DMA((1,)),
        ],
        compiler_params=pltpu.CompilerParams(vmem_limit_bytes=LIMIT),
        name="sweep",
    )(near(ga.reshape(2048, NX)), near(gb.reshape(2048, NX)), near(moved), far(starts))
    return new, change.reshape(())


def solution(mesh):
    return jax.shard_map(
        per_device,
        mesh=mesh,
        in_specs=(
            P("tm", "space", None, None),
            P("space", None, None),
            P("space", None, None),
            P("space", None, None),
            P("space", None, None),
        ),
        out_specs=(P("tm", "space", None, None), P()),
        check_vma=False,
    )
```

```python
import jax
import jax.numpy as jnp
from jax import lax
from jax.experimental import pallas as pl
from jax.experimental.pallas import tpu as pltpu
from jax.sharding import PartitionSpec as P


FSTEPS = 6
GC = 2
NZL, NY, NX = 12, 64, 128
SL = 16
SP = 16
NCELL = SL * 192 * NY * NX
COURANT = FSTEPS / (4.0 * GC)
DIFFUSE = FSTEPS / (16.0 * GC)

F32 = jnp.float32
LIMIT = 24 << 20
HBM = pl.BlockSpec(memory_space=pltpu.HBM)
VM = pl.BlockSpec(memory_space=pltpu.VMEM)


def near(x):
    return pltpu.with_memory_space_constraint(x, pltpu.VMEM)


def far(x):
    return pltpu.with_memory_space_constraint(x, pltpu.HBM)


def run_all(copies):
    for c in copies:
        c.start()
    for c in copies:
        c.wait()


def pack_kernel(st, vx, vy, vz, ka, pa, pb, sem):
    core = lax.rem(lax.axis_index("tm"), 2)
    odd = lax.rem(lax.axis_index("space"), 2)
    au, ac = 6 * (1 - odd), 7 * (1 - odd)
    bu, bc = 6 * odd, 7 * odd

    def go(f0, f1):
        pairs = [
            (st.at[0, pl.ds(au, 6)], pa.at[0:6]),
            (f0.at[pl.ds(ac, 5)], pa.at[6:11]),
            (f1.at[pl.ds(ac, 5)], pa.at[11:16]),
            (st.at[0, pl.ds(bu, 6)], pb.at[0:6]),
            (f0.at[pl.ds(bc, 5)], pb.at[6:11]),
            (f1.at[pl.ds(bc, 5)], pb.at[11:16]),
        ]
        run_all([pltpu.make_async_copy(a, b, sem.at[i]) for i, (a, b) in enumerate(pairs)])

    @pl.when(core == 0)
    def _():
        go(vx, vy)

    @pl.when(core == 1)
    def _():
        go(vz, ka)


def block_sum(v):
    row = lax.broadcasted_iota(jnp.int32, v.shape, 1)
    lane = lax.broadcasted_iota(jnp.int32, v.shape, 2)
    v = v + jnp.where((row & 1) == 0, pltpu.roll(v, 7, 1), pltpu.roll(v, 1, 1))
    v = v + jnp.where((row & 2) == 0, pltpu.roll(v, 6, 1), pltpu.roll(v, 2, 1))
    v = v + jnp.where((lane & 1) == 0, pltpu.roll(v, 127, 2), pltpu.roll(v, 1, 2))
    v = v + jnp.where((lane & 2) == 0, pltpu.roll(v, 126, 2), pltpu.roll(v, 2, 2))
    return v


def coarse_rows(m, rows, base):
    lane = lax.broadcasted_iota(jnp.int32, (8, NX), 1)
    for h in range(2):
        d = jnp.zeros((8, NX), F32)
        for q in range(4):
            d = d + jnp.where((lane & 3) == q, m[2 * q + h], 0.0)
        rows[base + 8 * h : base + 8 * h + 8, :] = d


def spread_lanes(rows):
    src = lax.broadcasted_iota(jnp.int32, (NX, NX), 0)
    dst = lax.broadcasted_iota(jnp.int32, (NX, NX), 1)
    perm = jnp.where(src == 4 * (dst & 31) + (dst >> 5), 1.0, 0.0).astype(F32)
    return jnp.dot(rows, perm, precision=lax.Precision.HIGHEST, preferred_element_type=F32)


def mix(v, before, after, w, i):
    x = w[1, i] * pltpu.roll(v, 1, 1) + w[2, i] * pltpu.roll(v, NX - 1, 1)
    y = w[3, i] * pltpu.roll(v, 1, 0) + w[4, i] * pltpu.roll(v, NY - 1, 0)
    z = w[5, i] * before + w[6, i] * after
    return w[0, i] * v + (x + (y + z))


def put_weights(w, i, cx, cy, cz, k):
    row = lax.broadcasted_iota(jnp.int32, (NY, NX), 0)
    lane = lax.broadcasted_iota(jnp.int32, (NY, NX), 1)
    xm, xp = k + jnp.maximum(cx, 0.0), k - jnp.minimum(cx, 0.0)
    ym, yp = k + jnp.maximum(cy, 0.0), k - jnp.minimum(cy, 0.0)
    zm, zp = k + jnp.maximum(cz, 0.0), k - jnp.minimum(cz, 0.0)
    w[0, i] = 1.0 - ((xm + xp) + (ym + yp) + (zm + zp))
    w[1, i] = jnp.where(lane == 0, 0.0, xm)
    w[2, i] = jnp.where(lane == NX - 1, 0.0, xp)
    w[3, i] = jnp.where(row == 0, 0.0, ym)
    w[4, i] = jnp.where(row == NY - 1, 0.0, yp)
    w[5, i] = zm
    w[6, i] = zp


def prep_kernel(st, vx, vy, vz, ka, w, lev, part, c, rows, ck, sem):
    n = lax.axis_index("tm")
    pairs = [(vx, c.at[0]), (vy, c.at[1]), (vz, c.at[2]), (ka, c.at[3]), (st.at[0], lev.at[0])]
    run_all([pltpu.make_async_copy(a, b, sem.at[i]) for i, (a, b) in enumerate(pairs)])

    def weights(i, _):
        put_weights(w, i, c[0, i], c[1, i], c[2, i], c[3, i])
        return 0

    lax.fori_loop(0, NZL, weights, 0, unroll=4)

    for t in range(1, FSTEPS):

        def plane(q, _, t=t):
            lev[t, q] = mix(lev[t - 1, q], lev[t - 1, q - 1], lev[t - 1, q + 1], w, q)
            return 0

        lax.fori_loop(t, NZL - t, plane, 0, unroll=NZL - 2 * t)

    f = n // 4
    scale = jnp.where(f < 3, COURANT / 64.0, DIFFUSE / 64.0).astype(F32)
    for zl in range(3):
        cs = [c[f, 4 * zl + i].reshape(8, 8, NX) for i in range(4)]
        coarse_rows(block_sum((cs[0] + cs[1]) + (cs[2] + cs[3])) * scale, rows, 16 * zl)
    ck[...] = spread_lanes(rows[...])
    for zl in range(3):
        part[zl : zl + 1, :] = ck[pl.ds(16 * zl + 4 * lax.rem(n, 4), 1), :]


def wedge(hi, own, other, w, lev, put, u, wk):
    first = lax.rem(lax.axis_index("tm"), 2) == 0
    sign = (1 - 2 * hi).astype(F32)

    def slab(k):
        return (k - 6) + hi * (23 - 2 * k)

    def halo(k, _):
        j = (k - 1) + hi * (6 - 2 * k)
        a0, a1, b0, b1 = own[6 + j], own[11 + j], other[6 + j], other[11 + j]
        put_weights(
            wk,
            k,
            jnp.where(first, a0, b0),
            jnp.where(first, a1, b1),
            jnp.where(first, b0, a0) * sign,
            jnp.where(first, b1, a1),
        )
        return 0

    def center(k, _):
        q = slab(k)
        for i in range(5):
            wk[i, k] = w[i, q]
        wk[5, k] = w[5 + hi, q]
        wk[6, k] = w[6 - hi, q]
        return 0

    lax.fori_loop(1, 6, halo, 0, unroll=5)
    lax.fori_loop(6, 12, center, 0, unroll=3)
    for k in range(6):
        u[0, k] = own[k + hi * (5 - 2 * k)]

    for t in range(1, FSTEPS + 1):
        a, b = (t - 1) % 2, t % 2
        for k in (5 + t, 6 + t):
            u[a, k] = lev[t - 1, slab(k)]

        def plane(k, _, a=a, b=b, t=t):
            new = mix(u[a, k], u[a, k - 1], u[a, k + 1], wk, k)
            if t == FSTEPS:
                put(k, slab(k), new)
            else:
                u[b, k] = new
            return 0

        lax.fori_loop(t, t + 6, plane, 0, unroll=6)
    return slab


def first_kernel(own, other, w, lev, half, u, wk):
    def put(k, q, new):
        half[k - 6] = new

    wedge(1 - lax.rem(lax.axis_index("space"), 2), own, other, w, lev, put, u, wk)


def second_kernel(own, other, w, lev, half, part, nx, fine, pay, u, wk, rows, ck):
    n = lax.axis_index("tm")
    hi = lax.rem(lax.axis_index("space"), 2)

    def put(k, q, new):
        fine[q] = new

    wedge(hi, own, other, w, lev, put, u, wk)
    for i in range(6):
        fine[i * (2 * hi - 1) + 11 * (1 - hi)] = half[i]

    live = jnp.where(n < SL - 1, 1.0, 0.0).astype(F32)
    var = jnp.zeros((8, NX), F32)
    for zl in range(3):
        ds = [(fine[4 * zl + i] - nx[4 * zl + i]).reshape(8, 8, NX) for i in range(4)]
        m = block_sum((ds[0] + ds[1]) + (ds[2] + ds[3])) * (1.0 / 64.0)
        for d in ds:
            r = d - m
            var = var + jnp.sum(r * r, axis=0)
        coarse_rows(m, rows, 16 * zl)
    ck[...] = spread_lanes(rows[...])
    for r in range(4):
        for zl in range(3):
            pay[0, r * 3 + zl : r * 3 + zl + 1, :] = ck[16 * zl + 4 * r : 16 * zl + 4 * r + 1, :]
    pay[0, 12:15, :] = part[0:3, :]
    pay[0, 15:16, :] = jnp.sum(var, axis=0, keepdims=True) * live
    for z in range(1, 8):
        pay[z] = pay[0]


def sweep_kernel(ga, gb, wide, change, w, gs, accs):
    core = lax.rem(lax.axis_index("tm"), 2)

    @pl.when(core == 0)
    def _():
        sweep(ga, gb, w, gs, accs)

    @pl.when(core == 1)
    def _():
        sweep(gb, ga, w, gs, accs)

    summary(wide, change, gs, accs)


def sweep(even, odd, w, gs, accs):
    def load(ref, z, q, h):
        return ref[pl.ds(h * 1024 + z * 16 + q, 8, stride=128), :]

    row = lax.broadcasted_iota(jnp.int32, (8, NX), 0)
    lane = lax.broadcasted_iota(jnp.int32, (8, NX), 1)
    x_lo, x_hi = (lane & 31) == 0, (lane & 31) == 31
    y_lo, y_hi = lane < 32, lane >= 96
    z_lo, z_hi = row == 0, row == 7

    def at(r, zl, h):
        return (r * 3 + zl) * 2 + h

    cells = [(r, zl, h) for r in range(4) for zl in range(3) for h in range(2)]
    for r, zl, h in cells:
        cx, cy, cz, k = (load((even, odd)[r % 2], 2 * f + r // 2, 12 + zl, h) for f in range(4))
        xm, xp = k + jnp.maximum(cx, 0.0), k - jnp.minimum(cx, 0.0)
        ym, yp = k + jnp.maximum(cy, 0.0), k - jnp.minimum(cy, 0.0)
        zm, zp = k + jnp.maximum(cz, 0.0), k - jnp.minimum(cz, 0.0)
        i = at(r, zl, h)
        w[0, i] = 1.0 - ((xm + xp) + (ym + yp) + (zm + zp))
        w[1, i] = jnp.where(x_lo, 0.0, xm)
        w[2, i] = jnp.where(x_hi, 0.0, xp)
        w[3, i] = jnp.where(y_lo, 0.0, ym) if r == 0 else ym
        w[4, i] = jnp.where(y_hi, 0.0, yp) if r == 3 else yp
        w[5, i] = jnp.where(z_lo, 0.0, zm) if zl == 0 and h == 0 else zm
        w[6, i] = jnp.where(z_hi, 0.0, zp) if zl == 2 and h == 1 else zp

    def coarse_step(e):
        new = []
        low = {}
        high = {}
        for r in range(4):
            dn = [pltpu.roll(e[at(r, 2, h)], 1, 0) for h in range(2)]
            low[r] = [dn[0], jnp.where(z_lo, dn[0], dn[1])]
            up = [pltpu.roll(e[at(r, 0, h)], 7, 0) for h in range(2)]
            high[r] = [jnp.where(z_hi, up[1], up[0]), up[1]]
        for r, zl, h in cells:
            i = at(r, zl, h)
            v = e[i]
            y0 = e[at(r - 1, zl, h)] if r > 0 else pltpu.roll(e[at(3, zl, h)], 32, 1)
            y1 = e[at(r + 1, zl, h)] if r < 3 else pltpu.roll(e[at(0, zl, h)], 96, 1)
            z0 = e[at(r, zl - 1, h)] if zl > 0 else low[r][h]
            z1 = e[at(r, zl + 1, h)] if zl < 2 else high[r][h]
            x = w[1, i] * pltpu.roll(v, 1, 1) + w[2, i] * pltpu.roll(v, NX - 1, 1)
            y = w[3, i] * y0 + w[4, i] * y1
            z = w[5, i] * z0 + w[6, i] * z1
            new.append(w[0, i] * v + (x + (y + z)))
        return tuple(new)

    e = tuple(load(even, 0, r * 3 + zl, h) for r, zl, h in cells)
    acc = jnp.zeros((8, NX), F32)
    for v in e:
        acc = acc + v * v
    for q in range(12):
        gs[0, q] = jnp.zeros((16, NX), F32)

    def turn(ref, z, n, e, acc):
        for _ in range(GC):
            e = coarse_step(e)
        new = []
        for r, zl, h in cells:
            g = e[at(r, zl, h)]
            gs[n, r * 3 + zl, 8 * h : 8 * h + 8, :] = g
            v = g + load(ref, z, r * 3 + zl, h)
            acc = acc + v * v
            new.append(v)
        return tuple(new), acc

    def two(z, carry):
        e, acc = turn(odd, z, 2 * z + 1, *carry)
        return turn(even, z + 1, 2 * z + 2, e, acc)

    e, acc = lax.fori_loop(0, 7, two, (e, acc))

    part = jnp.zeros((8, NX), F32)
    for ref in (even, odd):
        for b in range(16):
            part = part + ref[pl.ds(b * 128 + 15, 8, stride=16), :]
    accs[...] = part + 64.0 * acc


def summary(wide, change, gs, accs):
    nd = lax.axis_index("tm")
    s = lax.axis_index("space")
    value = jnp.sqrt(jnp.full((8, NX), jnp.sum(accs[...]) / NCELL, F32) + 1e-06)
    change[0, 0] = jnp.max(value)

    prev = jnp.maximum(nd - 1, 0)
    g12 = jnp.concatenate([gs[prev, q, pl.ds(s, 1), :] for q in range(12)] + [jnp.zeros((4, NX), F32)], axis=0)
    src = lax.broadcasted_iota(jnp.int32, (NX, 4 * NX), 0)
    dst = lax.broadcasted_iota(jnp.int32, (NX, 4 * NX), 1)
    spread = jnp.where(src == 32 * (dst >> 7) + ((dst & 127) >> 2), 1.0, 0.0).astype(F32)
    wide[...] = jnp.dot(g12, spread, precision=lax.Precision.HIGHEST, preferred_element_type=F32)


def finish_kernel(wide, fine, st, out, sem):
    nd = lax.axis_index("tm")
    row = lax.broadcasted_iota(jnp.int32, (8, NX), 0)

    @pl.when(nd == 0)
    def _():
        run_all([pltpu.make_async_copy(st.at[0], out.at[0], sem.at[0])])

    @pl.when(nd > 0)
    def _():
        for zl in range(3):
            for q in range(4):
                for h in range(2):
                    i0, i1 = 6 * h + zl, 6 * h + 3 + zl
                    lo = wide[i0 : i0 + 1, q * NX : (q + 1) * NX]
                    hi = wide[i1 : i1 + 1, q * NX : (q + 1) * NX]
                    tile = jnp.where(row < 4, jnp.broadcast_to(lo, (8, NX)), jnp.broadcast_to(hi, (8, NX)))
                    y = 8 * (2 * q + h)
                    for i in range(4):
                        out[0, 4 * zl + i, y : y + 8, :] = fine[4 * zl + i, y : y + 8, :] + tile


def per_device(starts, vel_x, vel_y, vel_z, kappa):
    plane = (NY, NX)
    shape = jax.ShapeDtypeStruct
    even = [(i, i ^ 1) for i in range(SP)]
    odd = [(i, i + 1) for i in range(1, SP - 1, 2)] + [(i + 1, i) for i in range(1, SP - 1, 2)]
    swap = [(i, i ^ 1) for i in range(SL)]
    down = [(i + 1, i) for i in range(SL - 1)]
    up = [(i, i + 1) for i in range(SL - 1)]
    zgroups = [[c + 2 * z for z in range(8)] for c in range(2)]

    pay_a, pay_b = pl.pallas_call(
        pack_kernel,
        out_shape=(pltpu.VMEM((16,) + plane, F32),) * 2,
        in_specs=[HBM] * 5,
        out_specs=(VM, VM),
        scratch_shapes=[pltpu.SemaphoreType.DMA((6,))],
        compiler_params=pltpu.CompilerParams(vmem_limit_bytes=LIMIT),
        name="pack",
    )(*(far(x) for x in (starts, vel_x, vel_y, vel_z, kappa)))
    rb = lax.ppermute(pay_b, "space", odd)
    ra = lax.ppermute(pay_a, "space", even)
    nxt = lax.ppermute(starts[0], "tm", down)
    w, lev, part = pl.pallas_call(
        prep_kernel,
        out_shape=(
            pltpu.VMEM((7, NZL) + plane, F32),
            pltpu.VMEM((FSTEPS, NZL) + plane, F32),
            pltpu.VMEM((8, NX), F32),
        ),
        in_specs=[HBM] * 5,
        out_specs=(VM, VM, VM),
        scratch_shapes=[
            pltpu.VMEM((4, NZL) + plane, F32),
            pltpu.VMEM((48, NX), F32),
            pltpu.VMEM((48, NX), F32),
            pltpu.SemaphoreType.DMA((5,)),
        ],
        compiler_params=pltpu.CompilerParams(vmem_limit_bytes=LIMIT),
        name="prep",
    )(*(far(x) for x in (starts, vel_x, vel_y, vel_z, kappa)))
    work = [pltpu.VMEM((2, 13) + plane, F32), pltpu.VMEM((7, 12) + plane, F32)]
    sa = lax.ppermute(ra, "tm", swap)
    half = pl.pallas_call(
        first_kernel,
        out_shape=pltpu.VMEM((6,) + plane, F32),
        in_specs=[VM] * 4,
        out_specs=VM,
        scratch_shapes=work,
        compiler_params=pltpu.CompilerParams(vmem_limit_bytes=LIMIT),
        name="first",
    )(near(ra), near(sa), near(w), near(lev))
    sb = lax.ppermute(rb, "tm", swap)
    fine, pay = pl.pallas_call(
        second_kernel,
        out_shape=(pltpu.VMEM((NZL,) + plane, F32), pltpu.VMEM((8, 16, NX), F32)),
        in_specs=[VM] * 7,
        out_specs=(VM, VM),
        scratch_shapes=work + [pltpu.VMEM((48, NX), F32), pltpu.VMEM((48, NX), F32)],
        compiler_params=pltpu.CompilerParams(vmem_limit_bytes=LIMIT),
        name="second",
    )(near(rb), near(sb), near(w), near(lev), near(half), near(part), near(nxt))

    gz = lax.all_to_all(pay, "tm", 0, 0, axis_index_groups=zgroups)
    moved = lax.ppermute(fine, "tm", up)
    ga = lax.all_to_all(jnp.broadcast_to(gz[None], (16, 8, 16, NX)), "space", 0, 0)
    gb = lax.ppermute(ga, "tm", swap)

    wide, change = pl.pallas_call(
        sweep_kernel,
        out_shape=(pltpu.VMEM((16, 4 * NX), F32), shape((1, 1), F32)),
        in_specs=[VM, VM],
        out_specs=(VM, pl.BlockSpec(memory_space=pltpu.SMEM)),
        scratch_shapes=[
            pltpu.VMEM((7, 24, 8, NX), F32),
            pltpu.VMEM((15, 12, 16, NX), F32),
            pltpu.VMEM((8, NX), F32),
        ],
        compiler_params=pltpu.CompilerParams(vmem_limit_bytes=LIMIT),
        name="sweep",
    )(near(ga.reshape(2048, NX)), near(gb.reshape(2048, NX)))
    new = pl.pallas_call(
        finish_kernel,
        out_shape=shape((1, NZL) + plane, F32),
        in_specs=[VM, VM, HBM],
        out_specs=VM,
        scratch_shapes=[pltpu.SemaphoreType.DMA((1,))],
        compiler_params=pltpu.CompilerParams(vmem_limit_bytes=LIMIT),
        name="finish",
    )(near(wide), near(moved), far(starts))
    return new, change.reshape(())


def solution(mesh):
    return jax.shard_map(
        per_device,
        mesh=mesh,
        in_specs=(
            P("tm", "space", None, None),
            P("space", None, None),
            P("space", None, None),
            P("space", None, None),
            P("space", None, None),
        ),
        out_specs=(P("tm", "space", None, None), P()),
        check_vma=False,
    )
```

```python
import jax
import jax.numpy as jnp
from jax import lax
from jax.experimental import pallas as pl
from jax.experimental.pallas import tpu as pltpu
from jax.sharding import PartitionSpec as P


FSTEPS = 6
GC = 2
NZL, NY, NX = 12, 64, 128
SL = 16
SP = 16
NCELL = SL * 192 * NY * NX
COURANT = FSTEPS / (4.0 * GC)
DIFFUSE = FSTEPS / (16.0 * GC)

F32 = jnp.float32
LIMIT = 24 << 20
HBM = pl.BlockSpec(memory_space=pltpu.HBM)
VM = pl.BlockSpec(memory_space=pltpu.VMEM)


def near(x):
    return pltpu.with_memory_space_constraint(x, pltpu.VMEM)


def far(x):
    return pltpu.with_memory_space_constraint(x, pltpu.HBM)


def run_all(copies):
    for c in copies:
        c.start()
    for c in copies:
        c.wait()


def pack_kernel(st, vx, vy, vz, ka, ca, cb, ha, hb, sem):
    core = lax.rem(lax.axis_index("tm"), 2)
    odd = lax.rem(lax.axis_index("space"), 2)
    au, ac = 6 * (1 - odd), 7 * (1 - odd)
    bu, bc = 6 * odd, 7 * odd

    def go(f0, f1):
        pairs = [
            (f0.at[pl.ds(ac, 5)], ca.at[0:5]),
            (f1.at[pl.ds(ac, 5)], ca.at[5:10]),
            (f0.at[pl.ds(bc, 5)], cb.at[0:5]),
            (f1.at[pl.ds(bc, 5)], cb.at[5:10]),
            (st.at[0, pl.ds(au, 6)], ha),
            (st.at[0, pl.ds(bu, 6)], hb),
        ]
        run_all([pltpu.make_async_copy(a, b, sem.at[i]) for i, (a, b) in enumerate(pairs)])

    @pl.when(core == 0)
    def _():
        go(vx, vy)

    @pl.when(core == 1)
    def _():
        go(vz, ka)


def block_sum(v):
    row = lax.broadcasted_iota(jnp.int32, v.shape, 1)
    lane = lax.broadcasted_iota(jnp.int32, v.shape, 2)
    v = v + jnp.where((row & 1) == 0, pltpu.roll(v, 7, 1), pltpu.roll(v, 1, 1))
    v = v + jnp.where((row & 2) == 0, pltpu.roll(v, 6, 1), pltpu.roll(v, 2, 1))
    v = v + jnp.where((lane & 1) == 0, pltpu.roll(v, 127, 2), pltpu.roll(v, 1, 2))
    v = v + jnp.where((lane & 2) == 0, pltpu.roll(v, 126, 2), pltpu.roll(v, 2, 2))
    return v


def coarse_rows(m, rows, base):
    lane = lax.broadcasted_iota(jnp.int32, (8, NX), 1)
    for h in range(2):
        d = jnp.zeros((8, NX), F32)
        for q in range(4):
            d = d + jnp.where((lane & 3) == q, m[2 * q + h], 0.0)
        rows[base + 8 * h : base + 8 * h + 8, :] = d


def spread_lanes(rows):
    src = lax.broadcasted_iota(jnp.int32, (NX, NX), 0)
    dst = lax.broadcasted_iota(jnp.int32, (NX, NX), 1)
    perm = jnp.where(src == 4 * (dst & 31) + (dst >> 5), 1.0, 0.0).astype(F32)
    return jnp.dot(rows, perm, precision=lax.Precision.HIGHEST, preferred_element_type=F32)


def mix(v, before, after, w, i):
    x = w[1, i] * pltpu.roll(v, 1, 1) + w[2, i] * pltpu.roll(v, NX - 1, 1)
    y = w[3, i] * pltpu.roll(v, 1, 0) + w[4, i] * pltpu.roll(v, NY - 1, 0)
    z = w[5, i] * before + w[6, i] * after
    return w[0, i] * v + (x + (y + z))


def put_weights(w, i, cx, cy, cz, k):
    row = lax.broadcasted_iota(jnp.int32, (NY, NX), 0)
    lane = lax.broadcasted_iota(jnp.int32, (NY, NX), 1)
    xm, xp = k + jnp.maximum(cx, 0.0), k - jnp.minimum(cx, 0.0)
    ym, yp = k + jnp.maximum(cy, 0.0), k - jnp.minimum(cy, 0.0)
    zm, zp = k + jnp.maximum(cz, 0.0), k - jnp.minimum(cz, 0.0)
    w[0, i] = 1.0 - ((xm + xp) + (ym + yp) + (zm + zp))
    w[1, i] = jnp.where(lane == 0, 0.0, xm)
    w[2, i] = jnp.where(lane == NX - 1, 0.0, xp)
    w[3, i] = jnp.where(row == 0, 0.0, ym)
    w[4, i] = jnp.where(row == NY - 1, 0.0, yp)
    w[5, i] = zm
    w[6, i] = zp


def prep_kernel(st, vx, vy, vz, ka, w, lev, part, c, rows, ck, sem):
    n = lax.axis_index("tm")
    pairs = [(vx, c.at[0]), (vy, c.at[1]), (vz, c.at[2]), (ka, c.at[3]), (st.at[0], lev.at[0])]
    run_all([pltpu.make_async_copy(a, b, sem.at[i]) for i, (a, b) in enumerate(pairs)])

    def weights(i, _):
        put_weights(w, i, c[0, i], c[1, i], c[2, i], c[3, i])
        return 0

    lax.fori_loop(0, NZL, weights, 0, unroll=4)

    for t in range(1, FSTEPS):

        def plane(q, _, t=t):
            lev[t, q] = mix(lev[t - 1, q], lev[t - 1, q - 1], lev[t - 1, q + 1], w, q)
            return 0

        lax.fori_loop(t, NZL - t, plane, 0, unroll=NZL - 2 * t)

    f = n // 4
    scale = jnp.where(f < 3, COURANT / 64.0, DIFFUSE / 64.0).astype(F32)
    for zl in range(3):
        cs = [c[f, 4 * zl + i].reshape(8, 8, NX) for i in range(4)]
        coarse_rows(block_sum((cs[0] + cs[1]) + (cs[2] + cs[3])) * scale, rows, 16 * zl)
    ck[...] = spread_lanes(rows[...])
    for zl in range(3):
        part[zl : zl + 1, :] = ck[pl.ds(16 * zl + 4 * lax.rem(n, 4), 1), :]


def wedge(hi, edge, own, other, w, lev, put, u, wk):
    first = lax.rem(lax.axis_index("tm"), 2) == 0
    sign = (1 - 2 * hi).astype(F32)

    def slab(k):
        return (k - 6) + hi * (23 - 2 * k)

    def halo(k, _):
        j = (k - 1) + hi * (6 - 2 * k)
        a0, a1, b0, b1 = own[j], own[5 + j], other[j], other[5 + j]
        put_weights(
            wk,
            k,
            jnp.where(first, a0, b0),
            jnp.where(first, a1, b1),
            jnp.where(first, b0, a0) * sign,
            jnp.where(first, b1, a1),
        )
        return 0

    def center(k, _):
        q = slab(k)
        for i in range(5):
            wk[i, k] = w[i, q]
        wk[5, k] = w[5 + hi, q]
        wk[6, k] = w[6 - hi, q]
        return 0

    lax.fori_loop(1, 6, halo, 0, unroll=5)
    lax.fori_loop(6, 12, center, 0, unroll=3)
    for k in range(6):
        u[0, k] = edge[k + hi * (5 - 2 * k)]

    for t in range(1, FSTEPS + 1):
        a, b = (t - 1) % 2, t % 2
        for k in (5 + t, 6 + t):
            u[a, k] = lev[t - 1, slab(k)]

        def plane(k, _, a=a, b=b, t=t):
            new = mix(u[a, k], u[a, k - 1], u[a, k + 1], wk, k)
            if t == FSTEPS:
                put(k, slab(k), new)
            else:
                u[b, k] = new
            return 0

        lax.fori_loop(t, t + 6, plane, 0, unroll=6)
    return slab


def first_kernel(edge, own, other, w, lev, half, u, wk):
    def put(k, q, new):
        half[k - 6] = new

    wedge(1 - lax.rem(lax.axis_index("space"), 2), edge, own, other, w, lev, put, u, wk)


def second_kernel(edge, own, other, w, lev, half, part, nx, fine, pay, u, wk, rows, ck):
    n = lax.axis_index("tm")
    hi = lax.rem(lax.axis_index("space"), 2)

    def put(k, q, new):
        fine[q] = new

    wedge(hi, edge, own, other, w, lev, put, u, wk)
    for i in range(6):
        fine[i * (2 * hi - 1) + 11 * (1 - hi)] = half[i]

    live = jnp.where(n < SL - 1, 1.0, 0.0).astype(F32)
    var = jnp.zeros((8, NX), F32)
    for zl in range(3):
        ds = [(fine[4 * zl + i] - nx[4 * zl + i]).reshape(8, 8, NX) for i in range(4)]
        m = block_sum((ds[0] + ds[1]) + (ds[2] + ds[3])) * (1.0 / 64.0)
        for d in ds:
            r = d - m
            var = var + jnp.sum(r * r, axis=0)
        coarse_rows(m, rows, 16 * zl)
    ck[...] = spread_lanes(rows[...])
    for r in range(4):
        for zl in range(3):
            pay[0, r * 3 + zl : r * 3 + zl + 1, :] = ck[16 * zl + 4 * r : 16 * zl + 4 * r + 1, :]
    pay[0, 12:15, :] = part[0:3, :]
    pay[0, 15:16, :] = jnp.sum(var, axis=0, keepdims=True) * live
    for z in range(1, 8):
        pay[z] = pay[0]


def sweep_kernel(ga, gb, wide, change, w, gs, accs):
    core = lax.rem(lax.axis_index("tm"), 2)

    @pl.when(core == 0)
    def _():
        sweep(ga, gb, w, gs, accs)

    @pl.when(core == 1)
    def _():
        sweep(gb, ga, w, gs, accs)

    summary(wide, change, gs, accs)


def sweep(even, odd, w, gs, accs):
    def load(ref, z, q, h):
        return ref[pl.ds(h * 1024 + z * 16 + q, 8, stride=128), :]

    row = lax.broadcasted_iota(jnp.int32, (8, NX), 0)
    lane = lax.broadcasted_iota(jnp.int32, (8, NX), 1)
    x_lo, x_hi = (lane & 31) == 0, (lane & 31) == 31
    y_lo, y_hi = lane < 32, lane >= 96
    z_lo, z_hi = row == 0, row == 7

    def at(r, zl, h):
        return (r * 3 + zl) * 2 + h

    cells = [(r, zl, h) for r in range(4) for zl in range(3) for h in range(2)]
    for r, zl, h in cells:
        cx, cy, cz, k = (load((even, odd)[r % 2], 2 * f + r // 2, 12 + zl, h) for f in range(4))
        xm, xp = k + jnp.maximum(cx, 0.0), k - jnp.minimum(cx, 0.0)
        ym, yp = k + jnp.maximum(cy, 0.0), k - jnp.minimum(cy, 0.0)
        zm, zp = k + jnp.maximum(cz, 0.0), k - jnp.minimum(cz, 0.0)
        i = at(r, zl, h)
        w[0, i] = 1.0 - ((xm + xp) + (ym + yp) + (zm + zp))
        w[1, i] = jnp.where(x_lo, 0.0, xm)
        w[2, i] = jnp.where(x_hi, 0.0, xp)
        w[3, i] = jnp.where(y_lo, 0.0, ym) if r == 0 else ym
        w[4, i] = jnp.where(y_hi, 0.0, yp) if r == 3 else yp
        w[5, i] = jnp.where(z_lo, 0.0, zm) if zl == 0 and h == 0 else zm
        w[6, i] = jnp.where(z_hi, 0.0, zp) if zl == 2 and h == 1 else zp

    def coarse_step(e):
        new = []
        low = {}
        high = {}
        for r in range(4):
            dn = [pltpu.roll(e[at(r, 2, h)], 1, 0) for h in range(2)]
            low[r] = [dn[0], jnp.where(z_lo, dn[0], dn[1])]
            up = [pltpu.roll(e[at(r, 0, h)], 7, 0) for h in range(2)]
            high[r] = [jnp.where(z_hi, up[1], up[0]), up[1]]
        for r, zl, h in cells:
            i = at(r, zl, h)
            v = e[i]
            y0 = e[at(r - 1, zl, h)] if r > 0 else pltpu.roll(e[at(3, zl, h)], 32, 1)
            y1 = e[at(r + 1, zl, h)] if r < 3 else pltpu.roll(e[at(0, zl, h)], 96, 1)
            z0 = e[at(r, zl - 1, h)] if zl > 0 else low[r][h]
            z1 = e[at(r, zl + 1, h)] if zl < 2 else high[r][h]
            x = w[1, i] * pltpu.roll(v, 1, 1) + w[2, i] * pltpu.roll(v, NX - 1, 1)
            y = w[3, i] * y0 + w[4, i] * y1
            z = w[5, i] * z0 + w[6, i] * z1
            new.append(w[0, i] * v + (x + (y + z)))
        return tuple(new)

    e = tuple(load(even, 0, r * 3 + zl, h) for r, zl, h in cells)
    acc = jnp.zeros((8, NX), F32)
    for v in e:
        acc = acc + v * v
    for q in range(12):
        gs[0, q] = jnp.zeros((16, NX), F32)

    def turn(ref, z, n, e, acc):
        for _ in range(GC):
            e = coarse_step(e)
        new = []
        for r, zl, h in cells:
            g = e[at(r, zl, h)]
            gs[n, r * 3 + zl, 8 * h : 8 * h + 8, :] = g
            v = g + load(ref, z, r * 3 + zl, h)
            acc = acc + v * v
            new.append(v)
        return tuple(new), acc

    def two(z, carry):
        e, acc = turn(odd, z, 2 * z + 1, *carry)
        return turn(even, z + 1, 2 * z + 2, e, acc)

    e, acc = lax.fori_loop(0, 7, two, (e, acc), unroll=7)

    part = jnp.zeros((8, NX), F32)
    for ref in (even, odd):
        for b in range(16):
            part = part + ref[pl.ds(b * 128 + 15, 8, stride=16), :]
    accs[...] = part + 64.0 * acc


def summary(wide, change, gs, accs):
    nd = lax.axis_index("tm")
    s = lax.axis_index("space")
    value = jnp.sqrt(jnp.full((8, NX), jnp.sum(accs[...]) / NCELL, F32) + 1e-06)
    change[0, 0] = jnp.max(value)

    prev = jnp.maximum(nd - 1, 0)
    g12 = jnp.concatenate([gs[prev, q, pl.ds(s, 1), :] for q in range(12)] + [jnp.zeros((4, NX), F32)], axis=0)
    src = lax.broadcasted_iota(jnp.int32, (NX, 4 * NX), 0)
    dst = lax.broadcasted_iota(jnp.int32, (NX, 4 * NX), 1)
    spread = jnp.where(src == 32 * (dst >> 7) + ((dst & 127) >> 2), 1.0, 0.0).astype(F32)
    wide[...] = jnp.dot(g12, spread, precision=lax.Precision.HIGHEST, preferred_element_type=F32)


def finish_kernel(wide, fine, st, out, sem):
    nd = lax.axis_index("tm")
    row = lax.broadcasted_iota(jnp.int32, (8, NX), 0)

    @pl.when(nd == 0)
    def _():
        run_all([pltpu.make_async_copy(st.at[0], out.at[0], sem.at[0])])

    @pl.when(nd > 0)
    def _():
        for zl in range(3):
            for q in range(4):
                for h in range(2):
                    i0, i1 = 6 * h + zl, 6 * h + 3 + zl
                    lo = wide[i0 : i0 + 1, q * NX : (q + 1) * NX]
                    hi = wide[i1 : i1 + 1, q * NX : (q + 1) * NX]
                    tile = jnp.where(row < 4, jnp.broadcast_to(lo, (8, NX)), jnp.broadcast_to(hi, (8, NX)))
                    y = 8 * (2 * q + h)
                    for i in range(4):
                        out[0, 4 * zl + i, y : y + 8, :] = fine[4 * zl + i, y : y + 8, :] + tile


def per_device(starts, vel_x, vel_y, vel_z, kappa):
    plane = (NY, NX)
    shape = jax.ShapeDtypeStruct
    even = [(i, i ^ 1) for i in range(SP)]
    odd = [(i, i + 1) for i in range(1, SP - 1, 2)] + [(i + 1, i) for i in range(1, SP - 1, 2)]
    swap = [(i, i ^ 1) for i in range(SL)]
    down = [(i + 1, i) for i in range(SL - 1)]
    up = [(i, i + 1) for i in range(SL - 1)]
    zgroups = [[c + 2 * z for z in range(8)] for c in range(2)]

    ca, cb, ha, hb = pl.pallas_call(
        pack_kernel,
        out_shape=(pltpu.VMEM((10,) + plane, F32),) * 2 + (pltpu.VMEM((6,) + plane, F32),) * 2,
        in_specs=[HBM] * 5,
        out_specs=(VM,) * 4,
        scratch_shapes=[pltpu.SemaphoreType.DMA((6,))],
        compiler_params=pltpu.CompilerParams(vmem_limit_bytes=LIMIT),
        name="pack",
    )(*(far(x) for x in (starts, vel_x, vel_y, vel_z, kappa)))
    ca = lax.ppermute(ca, "space", even)
    cb = lax.ppermute(cb, "space", odd)
    ha = lax.ppermute(ha, "space", even)
    hb = lax.ppermute(hb, "space", odd)
    nxt = lax.ppermute(starts[0], "tm", down)
    w, lev, part = pl.pallas_call(
        prep_kernel,
        out_shape=(
            pltpu.VMEM((7, NZL) + plane, F32),
            pltpu.VMEM((FSTEPS, NZL) + plane, F32),
            pltpu.VMEM((8, NX), F32),
        ),
        in_specs=[HBM] * 5,
        out_specs=(VM, VM, VM),
        scratch_shapes=[
            pltpu.VMEM((4, NZL) + plane, F32),
            pltpu.VMEM((48, NX), F32),
            pltpu.VMEM((48, NX), F32),
            pltpu.SemaphoreType.DMA((5,)),
        ],
        compiler_params=pltpu.CompilerParams(vmem_limit_bytes=LIMIT),
        name="prep",
    )(*(far(x) for x in (starts, vel_x, vel_y, vel_z, kappa)))
    work = [pltpu.VMEM((2, 13) + plane, F32), pltpu.VMEM((7, 12) + plane, F32)]
    sa = lax.ppermute(ca, "tm", swap)
    half = pl.pallas_call(
        first_kernel,
        out_shape=pltpu.VMEM((6,) + plane, F32),
        in_specs=[VM] * 5,
        out_specs=VM,
        scratch_shapes=work,
        compiler_params=pltpu.CompilerParams(vmem_limit_bytes=LIMIT),
        name="first",
    )(near(ha), near(ca), near(sa), near(w), near(lev))
    sb = lax.ppermute(cb, "tm", swap)
    fine, pay = pl.pallas_call(
        second_kernel,
        out_shape=(pltpu.VMEM((NZL,) + plane, F32), pltpu.VMEM((8, 16, NX), F32)),
        in_specs=[VM] * 8,
        out_specs=(VM, VM),
        scratch_shapes=work + [pltpu.VMEM((48, NX), F32), pltpu.VMEM((48, NX), F32)],
        compiler_params=pltpu.CompilerParams(vmem_limit_bytes=LIMIT),
        name="second",
    )(near(hb), near(cb), near(sb), near(w), near(lev), near(half), near(part), near(nxt))

    gz = lax.all_to_all(pay, "tm", 0, 0, axis_index_groups=zgroups)
    moved = lax.ppermute(fine, "tm", up)
    ga = lax.all_to_all(jnp.broadcast_to(gz[None], (16, 8, 16, NX)), "space", 0, 0)
    gb = lax.ppermute(ga, "tm", swap)

    wide, change = pl.pallas_call(
        sweep_kernel,
        out_shape=(pltpu.VMEM((16, 4 * NX), F32), shape((1, 1), F32)),
        in_specs=[VM, VM],
        out_specs=(VM, pl.BlockSpec(memory_space=pltpu.SMEM)),
        scratch_shapes=[
            pltpu.VMEM((7, 24, 8, NX), F32),
            pltpu.VMEM((15, 12, 16, NX), F32),
            pltpu.VMEM((8, NX), F32),
        ],
        compiler_params=pltpu.CompilerParams(vmem_limit_bytes=LIMIT),
        name="sweep",
    )(near(ga.reshape(2048, NX)), near(gb.reshape(2048, NX)))
    new = pl.pallas_call(
        finish_kernel,
        out_shape=shape((1, NZL) + plane, F32),
        in_specs=[VM, VM, HBM],
        out_specs=VM,
        scratch_shapes=[pltpu.SemaphoreType.DMA((1,))],
        compiler_params=pltpu.CompilerParams(vmem_limit_bytes=LIMIT),
        name="finish",
    )(near(wide), near(moved), far(starts))
    return new, change.reshape(())


def solution(mesh):
    return jax.shard_map(
        per_device,
        mesh=mesh,
        in_specs=(
            P("tm", "space", None, None),
            P("space", None, None),
            P("space", None, None),
            P("space", None, None),
            P("space", None, None),
        ),
        out_specs=(P("tm", "space", None, None), P()),
        check_vma=False,
    )
```

```python
import jax
import jax.numpy as jnp
from jax import lax
from jax.experimental import pallas as pl
from jax.experimental.pallas import tpu as pltpu
from jax.sharding import PartitionSpec as P


FSTEPS = 6
GC = 2
NZL, NY, NX = 12, 64, 128
SL = 16
SP = 16
NCELL = SL * 192 * NY * NX
COURANT = FSTEPS / (4.0 * GC)
DIFFUSE = FSTEPS / (16.0 * GC)

F32 = jnp.float32
LIMIT = 24 << 20
HBM = pl.BlockSpec(memory_space=pltpu.HBM)
VM = pl.BlockSpec(memory_space=pltpu.VMEM)


def near(x):
    return pltpu.with_memory_space_constraint(x, pltpu.VMEM)


def far(x):
    return pltpu.with_memory_space_constraint(x, pltpu.HBM)


def run_all(copies):
    for c in copies:
        c.start()
    for c in copies:
        c.wait()


def pack_kernel(st, vx, vy, vz, ka, ca, cb, ha, hb, sem):
    core = lax.rem(lax.axis_index("tm"), 2)
    odd = lax.rem(lax.axis_index("space"), 2)
    au, ac = 6 * (1 - odd), 7 * (1 - odd)
    bu, bc = 6 * odd, 7 * odd

    def go(f0, f1):
        pairs = [
            (f0.at[pl.ds(ac, 5)], ca.at[0:5]),
            (f1.at[pl.ds(ac, 5)], ca.at[5:10]),
            (f0.at[pl.ds(bc, 5)], cb.at[0:5]),
            (f1.at[pl.ds(bc, 5)], cb.at[5:10]),
            (st.at[0, pl.ds(au, 6)], ha),
            (st.at[0, pl.ds(bu, 6)], hb),
        ]
        run_all([pltpu.make_async_copy(a, b, sem.at[i]) for i, (a, b) in enumerate(pairs)])

    @pl.when(core == 0)
    def _():
        go(vx, vy)

    @pl.when(core == 1)
    def _():
        go(vz, ka)


def block_sum(v):
    row = lax.broadcasted_iota(jnp.int32, v.shape, 1)
    lane = lax.broadcasted_iota(jnp.int32, v.shape, 2)
    v = v + jnp.where((row & 1) == 0, pltpu.roll(v, 7, 1), pltpu.roll(v, 1, 1))
    v = v + jnp.where((row & 2) == 0, pltpu.roll(v, 6, 1), pltpu.roll(v, 2, 1))
    v = v + jnp.where((lane & 1) == 0, pltpu.roll(v, 127, 2), pltpu.roll(v, 1, 2))
    v = v + jnp.where((lane & 2) == 0, pltpu.roll(v, 126, 2), pltpu.roll(v, 2, 2))
    return v


def coarse_rows(m, rows, base):
    lane = lax.broadcasted_iota(jnp.int32, (8, NX), 1)
    for h in range(2):
        d = jnp.zeros((8, NX), F32)
        for q in range(4):
            d = d + jnp.where((lane & 3) == q, m[2 * q + h], 0.0)
        rows[base + 8 * h : base + 8 * h + 8, :] = d


def spread_lanes(rows):
    src = lax.broadcasted_iota(jnp.int32, (NX, NX), 0)
    dst = lax.broadcasted_iota(jnp.int32, (NX, NX), 1)
    perm = jnp.where(src == 4 * (dst & 31) + (dst >> 5), 1.0, 0.0).astype(F32)
    return jnp.dot(rows, perm, precision=lax.Precision.HIGHEST, preferred_element_type=F32)


def mix(v, before, after, w, i):
    x = w[1, i] * pltpu.roll(v, 1, 1) + w[2, i] * pltpu.roll(v, NX - 1, 1)
    y = w[3, i] * pltpu.roll(v, 1, 0) + w[4, i] * pltpu.roll(v, NY - 1, 0)
    z = w[5, i] * before + w[6, i] * after
    return w[0, i] * v + (x + (y + z))


def put_weights(w, i, cx, cy, cz, k):
    row = lax.broadcasted_iota(jnp.int32, (NY, NX), 0)
    lane = lax.broadcasted_iota(jnp.int32, (NY, NX), 1)
    xm, xp = k + jnp.maximum(cx, 0.0), k - jnp.minimum(cx, 0.0)
    ym, yp = k + jnp.maximum(cy, 0.0), k - jnp.minimum(cy, 0.0)
    zm, zp = k + jnp.maximum(cz, 0.0), k - jnp.minimum(cz, 0.0)
    w[0, i] = 1.0 - ((xm + xp) + (ym + yp) + (zm + zp))
    w[1, i] = jnp.where(lane == 0, 0.0, xm)
    w[2, i] = jnp.where(lane == NX - 1, 0.0, xp)
    w[3, i] = jnp.where(row == 0, 0.0, ym)
    w[4, i] = jnp.where(row == NY - 1, 0.0, yp)
    w[5, i] = zm
    w[6, i] = zp


def prep_kernel(st, vx, vy, vz, ka, w, lev, part, c, rows, ck, sem):
    n = lax.axis_index("tm")
    pairs = [(vx, c.at[0]), (vy, c.at[1]), (vz, c.at[2]), (ka, c.at[3]), (st.at[0], lev.at[0])]
    run_all([pltpu.make_async_copy(a, b, sem.at[i]) for i, (a, b) in enumerate(pairs)])

    def weights(i, _):
        put_weights(w, i, c[0, i], c[1, i], c[2, i], c[3, i])
        return 0

    lax.fori_loop(0, NZL, weights, 0, unroll=4)

    for t in range(1, FSTEPS):

        def plane(q, _, t=t):
            lev[t, q] = mix(lev[t - 1, q], lev[t - 1, q - 1], lev[t - 1, q + 1], w, q)
            return 0

        lax.fori_loop(t, NZL - t, plane, 0, unroll=NZL - 2 * t)

    f = n // 4
    scale = jnp.where(f < 3, COURANT / 64.0, DIFFUSE / 64.0).astype(F32)
    for zl in range(3):
        cs = [c[f, 4 * zl + i].reshape(8, 8, NX) for i in range(4)]
        coarse_rows(block_sum((cs[0] + cs[1]) + (cs[2] + cs[3])) * scale, rows, 16 * zl)
    ck[...] = spread_lanes(rows[...])
    for zl in range(3):
        part[zl : zl + 1, :] = ck[pl.ds(16 * zl + 4 * lax.rem(n, 4), 1), :]


def wedge(hi, edge, own, other, w, lev, put, u, wk):
    first = lax.rem(lax.axis_index("tm"), 2) == 0
    sign = (1 - 2 * hi).astype(F32)

    def slab(k):
        return (k - 6) + hi * (23 - 2 * k)

    def halo(k, _):
        j = (k - 1) + hi * (6 - 2 * k)
        a0, a1, b0, b1 = own[j], own[5 + j], other[j], other[5 + j]
        put_weights(
            wk,
            k,
            jnp.where(first, a0, b0),
            jnp.where(first, a1, b1),
            jnp.where(first, b0, a0) * sign,
            jnp.where(first, b1, a1),
        )
        return 0

    def center(k, _):
        q = slab(k)
        for i in range(5):
            wk[i, k] = w[i, q]
        wk[5, k] = w[5 + hi, q]
        wk[6, k] = w[6 - hi, q]
        return 0

    lax.fori_loop(1, 6, halo, 0, unroll=5)
    lax.fori_loop(6, 12, center, 0, unroll=3)
    for k in range(6):
        u[0, k] = edge[k + hi * (5 - 2 * k)]

    for t in range(1, FSTEPS + 1):
        a, b = (t - 1) % 2, t % 2
        for k in (5 + t, 6 + t):
            u[a, k] = lev[t - 1, slab(k)]

        def plane(k, _, a=a, b=b, t=t):
            new = mix(u[a, k], u[a, k - 1], u[a, k + 1], wk, k)
            if t == FSTEPS:
                put(k, slab(k), new)
            else:
                u[b, k] = new
            return 0

        lax.fori_loop(t, t + 6, plane, 0, unroll=6)
    return slab


def first_kernel(edge, own, other, w, lev, half, u, wk):
    def put(k, q, new):
        half[k - 6] = new

    wedge(1 - lax.rem(lax.axis_index("space"), 2), edge, own, other, w, lev, put, u, wk)


def second_kernel(edge, own, other, w, lev, half, part, nx, fine, pay, u, wk, rows, ck):
    n = lax.axis_index("tm")
    hi = lax.rem(lax.axis_index("space"), 2)

    def put(k, q, new):
        fine[q] = new

    wedge(hi, edge, own, other, w, lev, put, u, wk)
    for i in range(6):
        fine[i * (2 * hi - 1) + 11 * (1 - hi)] = half[i]

    live = jnp.where(n < SL - 1, 1.0, 0.0).astype(F32)
    var = jnp.zeros((8, NX), F32)
    for zl in range(3):
        ds = [(fine[4 * zl + i] - nx[4 * zl + i]).reshape(8, 8, NX) for i in range(4)]
        m = block_sum((ds[0] + ds[1]) + (ds[2] + ds[3])) * (1.0 / 64.0)
        for d in ds:
            r = d - m
            var = var + jnp.sum(r * r, axis=0)
        coarse_rows(m, rows, 16 * zl)
    ck[...] = spread_lanes(rows[...])
    for r in range(4):
        for zl in range(3):
            pay[0, r * 3 + zl : r * 3 + zl + 1, :] = ck[16 * zl + 4 * r : 16 * zl + 4 * r + 1, :]
    pay[0, 12:15, :] = part[0:3, :]
    pay[0, 15:16, :] = jnp.sum(var, axis=0, keepdims=True) * live
    for z in range(1, 8):
        pay[z] = pay[0]


def sweep_kernel(ga, gb, st, wide, change, kept, w, gs, accs, sem):
    nd = lax.axis_index("tm")
    core = lax.rem(nd, 2)
    keep = pltpu.make_async_copy(st.at[0], kept, sem.at[0])
    keep.start()

    @pl.when(core == 0)
    def _():
        sweep(ga, gb, w, gs, accs)

    @pl.when(core == 1)
    def _():
        sweep(gb, ga, w, gs, accs)

    summary(wide, change, gs, accs)
    keep.wait()


def sweep(even, odd, w, gs, accs):
    def load(ref, z, q, h):
        return ref[pl.ds(h * 1024 + z * 16 + q, 8, stride=128), :]

    row = lax.broadcasted_iota(jnp.int32, (8, NX), 0)
    lane = lax.broadcasted_iota(jnp.int32, (8, NX), 1)
    x_lo, x_hi = (lane & 31) == 0, (lane & 31) == 31
    y_lo, y_hi = lane < 32, lane >= 96
    z_lo, z_hi = row == 0, row == 7

    def at(r, zl, h):
        return (r * 3 + zl) * 2 + h

    cells = [(r, zl, h) for r in range(4) for zl in range(3) for h in range(2)]
    for r, zl, h in cells:
        cx, cy, cz, k = (load((even, odd)[r % 2], 2 * f + r // 2, 12 + zl, h) for f in range(4))
        xm, xp = k + jnp.maximum(cx, 0.0), k - jnp.minimum(cx, 0.0)
        ym, yp = k + jnp.maximum(cy, 0.0), k - jnp.minimum(cy, 0.0)
        zm, zp = k + jnp.maximum(cz, 0.0), k - jnp.minimum(cz, 0.0)
        i = at(r, zl, h)
        w[0, i] = 1.0 - ((xm + xp) + (ym + yp) + (zm + zp))
        w[1, i] = jnp.where(x_lo, 0.0, xm)
        w[2, i] = jnp.where(x_hi, 0.0, xp)
        w[3, i] = jnp.where(y_lo, 0.0, ym) if r == 0 else ym
        w[4, i] = jnp.where(y_hi, 0.0, yp) if r == 3 else yp
        w[5, i] = jnp.where(z_lo, 0.0, zm) if zl == 0 and h == 0 else zm
        w[6, i] = jnp.where(z_hi, 0.0, zp) if zl == 2 and h == 1 else zp

    def coarse_step(e):
        new = []
        low = {}
        high = {}
        for r in range(4):
            dn = [pltpu.roll(e[at(r, 2, h)], 1, 0) for h in range(2)]
            low[r] = [dn[0], jnp.where(z_lo, dn[0], dn[1])]
            up = [pltpu.roll(e[at(r, 0, h)], 7, 0) for h in range(2)]
            high[r] = [jnp.where(z_hi, up[1], up[0]), up[1]]
        for r, zl, h in cells:
            i = at(r, zl, h)
            v = e[i]
            y0 = e[at(r - 1, zl, h)] if r > 0 else pltpu.roll(e[at(3, zl, h)], 32, 1)
            y1 = e[at(r + 1, zl, h)] if r < 3 else pltpu.roll(e[at(0, zl, h)], 96, 1)
            z0 = e[at(r, zl - 1, h)] if zl > 0 else low[r][h]
            z1 = e[at(r, zl + 1, h)] if zl < 2 else high[r][h]
            x = w[1, i] * pltpu.roll(v, 1, 1) + w[2, i] * pltpu.roll(v, NX - 1, 1)
            y = w[3, i] * y0 + w[4, i] * y1
            z = w[5, i] * z0 + w[6, i] * z1
            new.append(w[0, i] * v + (x + (y + z)))
        return tuple(new)

    e = tuple(load(even, 0, r * 3 + zl, h) for r, zl, h in cells)
    acc = jnp.zeros((8, NX), F32)
    for v in e:
        acc = acc + v * v
    for q in range(12):
        gs[0, q] = jnp.zeros((16, NX), F32)

    def turn(ref, z, n, e, acc):
        for _ in range(GC):
            e = coarse_step(e)
        new = []
        for r, zl, h in cells:
            g = e[at(r, zl, h)]
            gs[n, r * 3 + zl, 8 * h : 8 * h + 8, :] = g
            v = g + load(ref, z, r * 3 + zl, h)
            acc = acc + v * v
            new.append(v)
        return tuple(new), acc

    def two(z, carry):
        e, acc = turn(odd, z, 2 * z + 1, *carry)
        return turn(even, z + 1, 2 * z + 2, e, acc)

    e, acc = lax.fori_loop(0, 7, two, (e, acc), unroll=7)

    part = jnp.zeros((8, NX), F32)
    for ref in (even, odd):
        for b in range(16):
            part = part + ref[pl.ds(b * 128 + 15, 8, stride=16), :]
    accs[...] = part + 64.0 * acc


def summary(wide, change, gs, accs):
    nd = lax.axis_index("tm")
    s = lax.axis_index("space")
    value = jnp.sqrt(jnp.full((8, NX), jnp.sum(accs[...]) / NCELL, F32) + 1e-06)
    change[0, 0] = jnp.max(value)

    prev = jnp.maximum(nd - 1, 0)
    g12 = jnp.concatenate([gs[prev, q, pl.ds(s, 1), :] for q in range(12)] + [jnp.zeros((4, NX), F32)], axis=0)
    src = lax.broadcasted_iota(jnp.int32, (NX, 4 * NX), 0)
    dst = lax.broadcasted_iota(jnp.int32, (NX, 4 * NX), 1)
    spread = jnp.where(src == 32 * (dst >> 7) + ((dst & 127) >> 2), 1.0, 0.0).astype(F32)
    wide[...] = jnp.dot(g12, spread, precision=lax.Precision.HIGHEST, preferred_element_type=F32)


def finish_kernel(wide, fine, kept, out):
    nd = lax.axis_index("tm")
    row = lax.broadcasted_iota(jnp.int32, (8, NX), 0)

    @pl.when(nd == 0)
    def _():
        for i in range(NZL):
            out[0, i] = kept[i]

    @pl.when(nd > 0)
    def _():
        for zl in range(3):
            for q in range(4):
                for h in range(2):
                    i0, i1 = 6 * h + zl, 6 * h + 3 + zl
                    lo = wide[i0 : i0 + 1, q * NX : (q + 1) * NX]
                    hi = wide[i1 : i1 + 1, q * NX : (q + 1) * NX]
                    tile = jnp.where(row < 4, jnp.broadcast_to(lo, (8, NX)), jnp.broadcast_to(hi, (8, NX)))
                    y = 8 * (2 * q + h)
                    for i in range(4):
                        out[0, 4 * zl + i, y : y + 8, :] = fine[4 * zl + i, y : y + 8, :] + tile


def per_device(starts, vel_x, vel_y, vel_z, kappa):
    plane = (NY, NX)
    shape = jax.ShapeDtypeStruct
    even = [(i, i ^ 1) for i in range(SP)]
    odd = [(i, i + 1) for i in range(1, SP - 1, 2)] + [(i + 1, i) for i in range(1, SP - 1, 2)]
    swap = [(i, i ^ 1) for i in range(SL)]
    down = [(i + 1, i) for i in range(SL - 1)]
    up = [(i, i + 1) for i in range(SL - 1)]
    zgroups = [[c + 2 * z for z in range(8)] for c in range(2)]

    ca, cb, ha, hb = pl.pallas_call(
        pack_kernel,
        out_shape=(pltpu.VMEM((10,) + plane, F32),) * 2 + (pltpu.VMEM((6,) + plane, F32),) * 2,
        in_specs=[HBM] * 5,
        out_specs=(VM,) * 4,
        scratch_shapes=[pltpu.SemaphoreType.DMA((6,))],
        compiler_params=pltpu.CompilerParams(vmem_limit_bytes=LIMIT),
        name="pack",
    )(*(far(x) for x in (starts, vel_x, vel_y, vel_z, kappa)))
    ca = lax.ppermute(ca, "space", even)
    cb = lax.ppermute(cb, "space", odd)
    ha = lax.ppermute(ha, "space", even)
    hb = lax.ppermute(hb, "space", odd)
    nxt = lax.ppermute(starts[0], "tm", down)
    w, lev, part = pl.pallas_call(
        prep_kernel,
        out_shape=(
            pltpu.VMEM((7, NZL) + plane, F32),
            pltpu.VMEM((FSTEPS, NZL) + plane, F32),
            pltpu.VMEM((8, NX), F32),
        ),
        in_specs=[HBM] * 5,
        out_specs=(VM, VM, VM),
        scratch_shapes=[
            pltpu.VMEM((4, NZL) + plane, F32),
            pltpu.VMEM((48, NX), F32),
            pltpu.VMEM((48, NX), F32),
            pltpu.SemaphoreType.DMA((5,)),
        ],
        compiler_params=pltpu.CompilerParams(vmem_limit_bytes=LIMIT),
        name="prep",
    )(*(far(x) for x in (starts, vel_x, vel_y, vel_z, kappa)))
    work = [pltpu.VMEM((2, 13) + plane, F32), pltpu.VMEM((7, 12) + plane, F32)]
    sa = lax.ppermute(ca, "tm", swap)
    half = pl.pallas_call(
        first_kernel,
        out_shape=pltpu.VMEM((6,) + plane, F32),
        in_specs=[VM] * 5,
        out_specs=VM,
        scratch_shapes=work,
        compiler_params=pltpu.CompilerParams(vmem_limit_bytes=LIMIT),
        name="first",
    )(near(ha), near(ca), near(sa), near(w), near(lev))
    sb = lax.ppermute(cb, "tm", swap)
    fine, pay = pl.pallas_call(
        second_kernel,
        out_shape=(pltpu.VMEM((NZL,) + plane, F32), pltpu.VMEM((8, 16, NX), F32)),
        in_specs=[VM] * 8,
        out_specs=(VM, VM),
        scratch_shapes=work + [pltpu.VMEM((48, NX), F32), pltpu.VMEM((48, NX), F32)],
        compiler_params=pltpu.CompilerParams(vmem_limit_bytes=LIMIT),
        name="second",
    )(near(hb), near(cb), near(sb), near(w), near(lev), near(half), near(part), near(nxt))

    gz = lax.all_to_all(pay, "tm", 0, 0, axis_index_groups=zgroups)
    moved = lax.ppermute(fine, "tm", up)
    ga = lax.all_to_all(jnp.broadcast_to(gz[None], (16, 8, 16, NX)), "space", 0, 0)
    gb = lax.ppermute(ga, "tm", swap)

    wide, change, kept = pl.pallas_call(
        sweep_kernel,
        out_shape=(pltpu.VMEM((16, 4 * NX), F32), shape((1, 1), F32), pltpu.VMEM((NZL,) + plane, F32)),
        in_specs=[VM, VM, HBM],
        out_specs=(VM, pl.BlockSpec(memory_space=pltpu.SMEM), VM),
        scratch_shapes=[
            pltpu.VMEM((7, 24, 8, NX), F32),
            pltpu.VMEM((15, 12, 16, NX), F32),
            pltpu.VMEM((8, NX), F32),
            pltpu.SemaphoreType.DMA((1,)),
        ],
        compiler_params=pltpu.CompilerParams(vmem_limit_bytes=LIMIT),
        name="sweep",
    )(near(ga.reshape(2048, NX)), near(gb.reshape(2048, NX)), far(starts))
    new = pl.pallas_call(
        finish_kernel,
        out_shape=shape((1, NZL) + plane, F32),
        in_specs=[VM, VM, VM],
        out_specs=VM,
        compiler_params=pltpu.CompilerParams(vmem_limit_bytes=LIMIT),
        name="finish",
    )(near(wide), near(moved), near(kept))
    return new, change.reshape(())


def solution(mesh):
    return jax.shard_map(
        per_device,
        mesh=mesh,
        in_specs=(
            P("tm", "space", None, None),
            P("space", None, None),
            P("space", None, None),
            P("space", None, None),
            P("space", None, None),
        ),
        out_specs=(P("tm", "space", None, None), P()),
        check_vma=False,
    )
```

```python
import jax
import jax.numpy as jnp
from jax import lax
from jax.experimental import pallas as pl
from jax.experimental.pallas import tpu as pltpu
from jax.sharding import PartitionSpec as P


FSTEPS = 6
GC = 2
NZL, NY, NX = 12, 64, 128
SL = 16
SP = 16
NCELL = SL * 192 * NY * NX
COURANT = FSTEPS / (4.0 * GC)
DIFFUSE = FSTEPS / (16.0 * GC)

F32 = jnp.float32
LIMIT = 24 << 20
HBM = pl.BlockSpec(memory_space=pltpu.HBM)
VM = pl.BlockSpec(memory_space=pltpu.VMEM)


def near(x):
    return pltpu.with_memory_space_constraint(x, pltpu.VMEM)


def far(x):
    return pltpu.with_memory_space_constraint(x, pltpu.HBM)


def run_all(copies):
    for c in copies:
        c.start()
    for c in copies:
        c.wait()


def pack_kernel(st, vx, vy, vz, ka, ca, cb, ha, hb, sem):
    core = lax.rem(lax.axis_index("tm"), 2)
    odd = lax.rem(lax.axis_index("space"), 2)
    au, ac = 6 * (1 - odd), 7 * (1 - odd)
    bu, bc = 6 * odd, 7 * odd

    def go(f0, f1):
        pairs = [
            (f0.at[pl.ds(ac, 5)], ca.at[0:5]),
            (f1.at[pl.ds(ac, 5)], ca.at[5:10]),
            (f0.at[pl.ds(bc, 5)], cb.at[0:5]),
            (f1.at[pl.ds(bc, 5)], cb.at[5:10]),
            (st.at[0, pl.ds(au, 6)], ha),
            (st.at[0, pl.ds(bu, 6)], hb),
        ]
        run_all([pltpu.make_async_copy(a, b, sem.at[i]) for i, (a, b) in enumerate(pairs)])

    @pl.when(core == 0)
    def _():
        go(vx, vy)

    @pl.when(core == 1)
    def _():
        go(vz, ka)


def block_sum(v):
    row = lax.broadcasted_iota(jnp.int32, v.shape, 1)
    lane = lax.broadcasted_iota(jnp.int32, v.shape, 2)
    v = v + jnp.where((row & 1) == 0, pltpu.roll(v, 7, 1), pltpu.roll(v, 1, 1))
    v = v + jnp.where((row & 2) == 0, pltpu.roll(v, 6, 1), pltpu.roll(v, 2, 1))
    v = v + jnp.where((lane & 1) == 0, pltpu.roll(v, 127, 2), pltpu.roll(v, 1, 2))
    v = v + jnp.where((lane & 2) == 0, pltpu.roll(v, 126, 2), pltpu.roll(v, 2, 2))
    return v


def coarse_rows(m, rows, base):
    lane = lax.broadcasted_iota(jnp.int32, (8, NX), 1)
    for h in range(2):
        d = jnp.zeros((8, NX), F32)
        for q in range(4):
            d = d + jnp.where((lane & 3) == q, m[2 * q + h], 0.0)
        rows[base + 8 * h : base + 8 * h + 8, :] = d


def spread_lanes(rows):
    src = lax.broadcasted_iota(jnp.int32, (NX, NX), 0)
    dst = lax.broadcasted_iota(jnp.int32, (NX, NX), 1)
    perm = jnp.where(src == 4 * (dst & 31) + (dst >> 5), 1.0, 0.0).astype(F32)
    return jnp.dot(rows, perm, precision=lax.Precision.HIGHEST, preferred_element_type=F32)


def mix(v, before, after, w, i):
    x = w[1, i] * pltpu.roll(v, 1, 1) + w[2, i] * pltpu.roll(v, NX - 1, 1)
    y = w[3, i] * pltpu.roll(v, 1, 0) + w[4, i] * pltpu.roll(v, NY - 1, 0)
    z = w[5, i] * before + w[6, i] * after
    return w[0, i] * v + (x + (y + z))


def put_weights(w, i, cx, cy, cz, k):
    row = lax.broadcasted_iota(jnp.int32, (NY, NX), 0)
    lane = lax.broadcasted_iota(jnp.int32, (NY, NX), 1)
    xm, xp = k + jnp.maximum(cx, 0.0), k - jnp.minimum(cx, 0.0)
    ym, yp = k + jnp.maximum(cy, 0.0), k - jnp.minimum(cy, 0.0)
    zm, zp = k + jnp.maximum(cz, 0.0), k - jnp.minimum(cz, 0.0)
    w[0, i] = 1.0 - ((xm + xp) + (ym + yp) + (zm + zp))
    w[1, i] = jnp.where(lane == 0, 0.0, xm)
    w[2, i] = jnp.where(lane == NX - 1, 0.0, xp)
    w[3, i] = jnp.where(row == 0, 0.0, ym)
    w[4, i] = jnp.where(row == NY - 1, 0.0, yp)
    w[5, i] = zm
    w[6, i] = zp


def prep_kernel(st, vx, vy, vz, ka, w, lev, part, c, rows, ck, sem):
    n = lax.axis_index("tm")
    pairs = [(vx, c.at[0]), (vy, c.at[1]), (vz, c.at[2]), (ka, c.at[3]), (st.at[0], lev.at[0])]
    run_all([pltpu.make_async_copy(a, b, sem.at[i]) for i, (a, b) in enumerate(pairs)])

    def weights(i, _):
        put_weights(w, i, c[0, i], c[1, i], c[2, i], c[3, i])
        return 0

    lax.fori_loop(0, NZL, weights, 0, unroll=4)

    for t in range(1, FSTEPS):

        def plane(q, _, t=t):
            lev[t, q] = mix(lev[t - 1, q], lev[t - 1, q - 1], lev[t - 1, q + 1], w, q)
            return 0

        lax.fori_loop(t, NZL - t, plane, 0, unroll=NZL - 2 * t)

    f = n // 4
    scale = jnp.where(f < 3, COURANT / 64.0, DIFFUSE / 64.0).astype(F32)
    for zl in range(3):
        cs = [c[f, 4 * zl + i].reshape(8, 8, NX) for i in range(4)]
        coarse_rows(block_sum((cs[0] + cs[1]) + (cs[2] + cs[3])) * scale, rows, 16 * zl)
    ck[...] = spread_lanes(rows[...])
    for zl in range(3):
        part[zl : zl + 1, :] = ck[pl.ds(16 * zl + 4 * lax.rem(n, 4), 1), :]


def wedge(hi, edge, own, other, w, lev, put, u, wk):
    first = lax.rem(lax.axis_index("tm"), 2) == 0
    sign = (1 - 2 * hi).astype(F32)

    def slab(k):
        return (k - 6) + hi * (23 - 2 * k)

    def halo(k, _):
        j = (k - 1) + hi * (6 - 2 * k)
        a0, a1, b0, b1 = own[j], own[5 + j], other[j], other[5 + j]
        put_weights(
            wk,
            k,
            jnp.where(first, a0, b0),
            jnp.where(first, a1, b1),
            jnp.where(first, b0, a0) * sign,
            jnp.where(first, b1, a1),
        )
        return 0

    def center(k, _):
        q = slab(k)
        for i in range(5):
            wk[i, k] = w[i, q]
        wk[5, k] = w[5 + hi, q]
        wk[6, k] = w[6 - hi, q]
        return 0

    lax.fori_loop(1, 6, halo, 0, unroll=5)
    lax.fori_loop(6, 12, center, 0, unroll=3)
    for k in range(6):
        u[0, k] = edge[k + hi * (5 - 2 * k)]

    for t in range(1, FSTEPS + 1):
        a, b = (t - 1) % 2, t % 2
        for k in (5 + t, 6 + t):
            u[a, k] = lev[t - 1, slab(k)]

        def plane(k, _, a=a, b=b, t=t):
            new = mix(u[a, k], u[a, k - 1], u[a, k + 1], wk, k)
            if t == FSTEPS:
                put(k, slab(k), new)
            else:
                u[b, k] = new
            return 0

        lax.fori_loop(t, t + 6, plane, 0, unroll=6)
    return slab


def first_kernel(edge, own, other, w, lev, half, u, wk):
    def put(k, q, new):
        half[k - 6] = new

    wedge(lax.rem(lax.axis_index("space"), 2), edge, own, other, w, lev, put, u, wk)


def second_kernel(edge, own, other, w, lev, half, part, nx, fine, pay, u, wk, rows, ck):
    n = lax.axis_index("tm")
    hi = 1 - lax.rem(lax.axis_index("space"), 2)

    def put(k, q, new):
        fine[q] = new

    wedge(hi, edge, own, other, w, lev, put, u, wk)
    for i in range(6):
        fine[i * (2 * hi - 1) + 11 * (1 - hi)] = half[i]

    live = jnp.where(n < SL - 1, 1.0, 0.0).astype(F32)
    var = jnp.zeros((8, NX), F32)
    for zl in range(3):
        ds = [(fine[4 * zl + i] - nx[4 * zl + i]).reshape(8, 8, NX) for i in range(4)]
        m = block_sum((ds[0] + ds[1]) + (ds[2] + ds[3])) * (1.0 / 64.0)
        for d in ds:
            r = d - m
            var = var + jnp.sum(r * r, axis=0)
        coarse_rows(m, rows, 16 * zl)
    ck[...] = spread_lanes(rows[...])
    for r in range(4):
        for zl in range(3):
            pay[0, r * 3 + zl : r * 3 + zl + 1, :] = ck[16 * zl + 4 * r : 16 * zl + 4 * r + 1, :]
    pay[0, 12:15, :] = part[0:3, :]
    pay[0, 15:16, :] = jnp.sum(var, axis=0, keepdims=True) * live
    for z in range(1, 8):
        pay[z] = pay[0]


def sweep_kernel(ga, gb, st, wide, change, kept, w, gs, accs, sem):
    nd = lax.axis_index("tm")
    core = lax.rem(nd, 2)
    keep = pltpu.make_async_copy(st.at[0], kept, sem.at[0])
    keep.start()

    @pl.when(core == 0)
    def _():
        sweep(ga, gb, w, gs, accs)

    @pl.when(core == 1)
    def _():
        sweep(gb, ga, w, gs, accs)

    summary(wide, change, gs, accs)
    keep.wait()


def sweep(even, odd, w, gs, accs):
    def load(ref, z, q, h):
        return ref[pl.ds(h * 1024 + z * 16 + q, 8, stride=128), :]

    row = lax.broadcasted_iota(jnp.int32, (8, NX), 0)
    lane = lax.broadcasted_iota(jnp.int32, (8, NX), 1)
    x_lo, x_hi = (lane & 31) == 0, (lane & 31) == 31
    y_lo, y_hi = lane < 32, lane >= 96
    z_lo, z_hi = row == 0, row == 7

    def at(r, zl, h):
        return (r * 3 + zl) * 2 + h

    cells = [(r, zl, h) for r in range(4) for zl in range(3) for h in range(2)]
    for r, zl, h in cells:
        cx, cy, cz, k = (load((even, odd)[r % 2], 2 * f + r // 2, 12 + zl, h) for f in range(4))
        xm, xp = k + jnp.maximum(cx, 0.0), k - jnp.minimum(cx, 0.0)
        ym, yp = k + jnp.maximum(cy, 0.0), k - jnp.minimum(cy, 0.0)
        zm, zp = k + jnp.maximum(cz, 0.0), k - jnp.minimum(cz, 0.0)
        i = at(r, zl, h)
        w[0, i] = 1.0 - ((xm + xp) + (ym + yp) + (zm + zp))
        w[1, i] = jnp.where(x_lo, 0.0, xm)
        w[2, i] = jnp.where(x_hi, 0.0, xp)
        w[3, i] = jnp.where(y_lo, 0.0, ym) if r == 0 else ym
        w[4, i] = jnp.where(y_hi, 0.0, yp) if r == 3 else yp
        w[5, i] = jnp.where(z_lo, 0.0, zm) if zl == 0 and h == 0 else zm
        w[6, i] = jnp.where(z_hi, 0.0, zp) if zl == 2 and h == 1 else zp

    def coarse_step(e):
        new = []
        low = {}
        high = {}
        for r in range(4):
            dn = [pltpu.roll(e[at(r, 2, h)], 1, 0) for h in range(2)]
            low[r] = [dn[0], jnp.where(z_lo, dn[0], dn[1])]
            up = [pltpu.roll(e[at(r, 0, h)], 7, 0) for h in range(2)]
            high[r] = [jnp.where(z_hi, up[1], up[0]), up[1]]
        for r, zl, h in cells:
            i = at(r, zl, h)
            v = e[i]
            y0 = e[at(r - 1, zl, h)] if r > 0 else pltpu.roll(e[at(3, zl, h)], 32, 1)
            y1 = e[at(r + 1, zl, h)] if r < 3 else pltpu.roll(e[at(0, zl, h)], 96, 1)
            z0 = e[at(r, zl - 1, h)] if zl > 0 else low[r][h]
            z1 = e[at(r, zl + 1, h)] if zl < 2 else high[r][h]
            x = w[1, i] * pltpu.roll(v, 1, 1) + w[2, i] * pltpu.roll(v, NX - 1, 1)
            y = w[3, i] * y0 + w[4, i] * y1
            z = w[5, i] * z0 + w[6, i] * z1
            new.append(w[0, i] * v + (x + (y + z)))
        return tuple(new)

    e = tuple(load(even, 0, r * 3 + zl, h) for r, zl, h in cells)
    acc = jnp.zeros((8, NX), F32)
    for v in e:
        acc = acc + v * v
    for q in range(12):
        gs[0, q] = jnp.zeros((16, NX), F32)

    def turn(ref, z, n, e, acc):
        for _ in range(GC):
            e = coarse_step(e)
        new = []
        for r, zl, h in cells:
            g = e[at(r, zl, h)]
            gs[n, r * 3 + zl, 8 * h : 8 * h + 8, :] = g
            v = g + load(ref, z, r * 3 + zl, h)
            acc = acc + v * v
            new.append(v)
        return tuple(new), acc

    def two(z, carry):
        e, acc = turn(odd, z, 2 * z + 1, *carry)
        return turn(even, z + 1, 2 * z + 2, e, acc)

    e, acc = lax.fori_loop(0, 7, two, (e, acc), unroll=7)

    part = jnp.zeros((8, NX), F32)
    for ref in (even, odd):
        for b in range(16):
            part = part + ref[pl.ds(b * 128 + 15, 8, stride=16), :]
    accs[...] = part + 64.0 * acc


def summary(wide, change, gs, accs):
    nd = lax.axis_index("tm")
    s = lax.axis_index("space")
    value = jnp.sqrt(jnp.full((8, NX), jnp.sum(accs[...]) / NCELL, F32) + 1e-06)
    change[0, 0] = jnp.max(value)

    prev = jnp.maximum(nd - 1, 0)
    g12 = jnp.concatenate([gs[prev, q, pl.ds(s, 1), :] for q in range(12)] + [jnp.zeros((4, NX), F32)], axis=0)
    src = lax.broadcasted_iota(jnp.int32, (NX, 4 * NX), 0)
    dst = lax.broadcasted_iota(jnp.int32, (NX, 4 * NX), 1)
    spread = jnp.where(src == 32 * (dst >> 7) + ((dst & 127) >> 2), 1.0, 0.0).astype(F32)
    wide[...] = jnp.dot(g12, spread, precision=lax.Precision.HIGHEST, preferred_element_type=F32)


def finish_kernel(wide, fine, kept, out):
    nd = lax.axis_index("tm")
    row = lax.broadcasted_iota(jnp.int32, (8, NX), 0)

    @pl.when(nd == 0)
    def _():
        for i in range(NZL):
            out[0, i] = kept[i]

    @pl.when(nd > 0)
    def _():
        for zl in range(3):
            for q in range(4):
                for h in range(2):
                    i0, i1 = 6 * h + zl, 6 * h + 3 + zl
                    lo = wide[i0 : i0 + 1, q * NX : (q + 1) * NX]
                    hi = wide[i1 : i1 + 1, q * NX : (q + 1) * NX]
                    tile = jnp.where(row < 4, jnp.broadcast_to(lo, (8, NX)), jnp.broadcast_to(hi, (8, NX)))
                    y = 8 * (2 * q + h)
                    for i in range(4):
                        out[0, 4 * zl + i, y : y + 8, :] = fine[4 * zl + i, y : y + 8, :] + tile


def per_device(starts, vel_x, vel_y, vel_z, kappa):
    plane = (NY, NX)
    shape = jax.ShapeDtypeStruct
    even = [(i, i ^ 1) for i in range(SP)]
    odd = [(i, i + 1) for i in range(1, SP - 1, 2)] + [(i + 1, i) for i in range(1, SP - 1, 2)]
    swap = [(i, i ^ 1) for i in range(SL)]
    down = [(i + 1, i) for i in range(SL - 1)]
    up = [(i, i + 1) for i in range(SL - 1)]
    zgroups = [[c + 2 * z for z in range(8)] for c in range(2)]

    ca, cb, ha, hb = pl.pallas_call(
        pack_kernel,
        out_shape=(pltpu.VMEM((10,) + plane, F32),) * 2 + (pltpu.VMEM((6,) + plane, F32),) * 2,
        in_specs=[HBM] * 5,
        out_specs=(VM,) * 4,
        scratch_shapes=[pltpu.SemaphoreType.DMA((6,))],
        compiler_params=pltpu.CompilerParams(vmem_limit_bytes=LIMIT),
        name="pack",
    )(*(far(x) for x in (starts, vel_x, vel_y, vel_z, kappa)))
    ca = lax.ppermute(ca, "space", even)
    cb = lax.ppermute(cb, "space", odd)
    ha = lax.ppermute(ha, "space", even)
    hb = lax.ppermute(hb, "space", odd)
    nxt = lax.ppermute(starts[0], "tm", down)
    w, lev, part = pl.pallas_call(
        prep_kernel,
        out_shape=(
            pltpu.VMEM((7, NZL) + plane, F32),
            pltpu.VMEM((FSTEPS, NZL) + plane, F32),
            pltpu.VMEM((8, NX), F32),
        ),
        in_specs=[HBM] * 5,
        out_specs=(VM, VM, VM),
        scratch_shapes=[
            pltpu.VMEM((4, NZL) + plane, F32),
            pltpu.VMEM((48, NX), F32),
            pltpu.VMEM((48, NX), F32),
            pltpu.SemaphoreType.DMA((5,)),
        ],
        compiler_params=pltpu.CompilerParams(vmem_limit_bytes=LIMIT),
        name="prep",
    )(*(far(x) for x in (starts, vel_x, vel_y, vel_z, kappa)))
    work = [pltpu.VMEM((2, 13) + plane, F32), pltpu.VMEM((7, 12) + plane, F32)]
    sa = lax.ppermute(ca, "tm", swap)
    sb = lax.ppermute(cb, "tm", swap)
    half = pl.pallas_call(
        first_kernel,
        out_shape=pltpu.VMEM((6,) + plane, F32),
        in_specs=[VM] * 5,
        out_specs=VM,
        scratch_shapes=work,
        compiler_params=pltpu.CompilerParams(vmem_limit_bytes=LIMIT),
        name="first",
    )(near(hb), near(cb), near(sb), near(w), near(lev))
    fine, pay = pl.pallas_call(
        second_kernel,
        out_shape=(pltpu.VMEM((NZL,) + plane, F32), pltpu.VMEM((8, 16, NX), F32)),
        in_specs=[VM] * 8,
        out_specs=(VM, VM),
        scratch_shapes=work + [pltpu.VMEM((48, NX), F32), pltpu.VMEM((48, NX), F32)],
        compiler_params=pltpu.CompilerParams(vmem_limit_bytes=LIMIT),
        name="second",
    )(near(ha), near(ca), near(sa), near(w), near(lev), near(half), near(part), near(nxt))

    gz = lax.all_to_all(pay, "tm", 0, 0, axis_index_groups=zgroups)
    moved = lax.ppermute(fine, "tm", up)
    ga = lax.all_to_all(jnp.broadcast_to(gz[None], (16, 8, 16, NX)), "space", 0, 0)
    gb = lax.ppermute(ga, "tm", swap)

    wide, change, kept = pl.pallas_call(
        sweep_kernel,
        out_shape=(pltpu.VMEM((16, 4 * NX), F32), shape((1, 1), F32), pltpu.VMEM((NZL,) + plane, F32)),
        in_specs=[VM, VM, HBM],
        out_specs=(VM, pl.BlockSpec(memory_space=pltpu.SMEM), VM),
        scratch_shapes=[
            pltpu.VMEM((7, 24, 8, NX), F32),
            pltpu.VMEM((15, 12, 16, NX), F32),
            pltpu.VMEM((8, NX), F32),
            pltpu.SemaphoreType.DMA((1,)),
        ],
        compiler_params=pltpu.CompilerParams(vmem_limit_bytes=LIMIT),
        name="sweep",
    )(near(ga.reshape(2048, NX)), near(gb.reshape(2048, NX)), far(starts))
    new = pl.pallas_call(
        finish_kernel,
        out_shape=shape((1, NZL) + plane, F32),
        in_specs=[VM, VM, VM],
        out_specs=VM,
        compiler_params=pltpu.CompilerParams(vmem_limit_bytes=LIMIT),
        name="finish",
    )(near(wide), near(moved), near(kept))
    return new, change.reshape(())


def solution(mesh):
    return jax.shard_map(
        per_device,
        mesh=mesh,
        in_specs=(
            P("tm", "space", None, None),
            P("space", None, None),
            P("space", None, None),
            P("space", None, None),
            P("space", None, None),
        ),
        out_specs=(P("tm", "space", None, None), P()),
        check_vma=False,
    )
```
